256 devices in a mesh: tm: 8 (over y, x_lo), space: 32 (over z, x_hi, core).
Axes of the slice: x: 4 (x_hi: 2, x_lo: 2; x = x_hi * 2 + x_lo), y: 4, z: 8, core: 2. Of those that a mesh axis runs over, the one named last changes fastest.
Arguments:
- starts: float32 [8, 256, 256, 128], P('tm', 'space'), may hold values from -6 to 6
- material: int32 [256, 256, 128], P('space'), may hold values from 0 to 7, as said below
- source: float32 [256, 256, 128], P('space'), may hold values from -6 to 6
Outputs:
- next_starts: float32 [8, 256, 256, 128], P('tm', 'space')
The draws below stay inside these ranges and needn't reach their ends.
Inputs may be any that keep to these rules, and one draw needn't show every extreme that they name: `material`: index into the table of 8 conductivities.
All inputs are finite; a program needn't handle non-finite values.
Results may differ from the reference program's by a relative error of at most 0.0001.
Values sent between devices are 32-bit elements; how exact they have to be, the bound alone decides.
No kernel may reach another device: no remote copies, remote signals or barrier semaphores. Data moves between devices by JAX's collectives and lax.ppermute only.
A program may use at most 64 MiB of HBM per device.

```python
import jax
import jax.numpy as jnp

NY = 256
NZ = 128
FSTEPS = 4
CSTEPS = 2
ITERS = 1
NT = 8
NX = 256
N_TM = 8


def draw_material(key, part):
    key_base, key_pick, key_spot = jax.random.split(key, 3)
    shape = (NX, NY, NZ)
    total = NX * NY * NZ
    base = jax.random.randint(key_base, shape, 0, 8, dtype=jnp.int32)
    pick = jax.random.randint(key_pick, shape, 0, 8, dtype=jnp.int32)
    values = jnp.where(pick < 7, jnp.int32(0), base)
    spot = jax.random.randint(key_spot, (), 0, total - 1, dtype=jnp.int32)
    flat = jnp.arange(total, dtype=jnp.int32).reshape(shape)
    values = jnp.where(flat == spot, jnp.int32(7), values)
    values = jnp.where(flat == spot + 1, jnp.int32(0), values)
    return values.astype(jnp.int32)


def block_scale(own_key, shape, cuts, least, high):
    factor_of = 1.0
    for dim, blocks in cuts:
        heights = jax.random.uniform(jax.random.fold_in(jax.random.fold_in(own_key, 6), dim), (blocks,), jnp.float32, least / len(cuts), high / len(cuts))
        factor_of = factor_of * jnp.repeat(jnp.exp(heights), shape[dim] // blocks).reshape((-1,) + (1,) * (len(shape) - 1 - dim))
    return factor_of


def gaussian(rng, extent, scale, reach, pieces=(), kind=jnp.bfloat16):
    values = scale * jax.random.normal(rng, extent, jnp.float32)
    if pieces:
        values = values * block_scale(rng, extent, pieces, -0.22, 0.18)
    return jnp.clip(values, -reach, reach).astype(kind)


def setup_inputs(seed: int = 0) -> dict:
    seeds = jax.random.split(jax.random.key(seed), 4)
    return {
        "starts": gaussian(seeds[0], (NT, NX, NY, NZ), 1.0, 6.0, ((0, 8), (1, 32)), jnp.float32),
        "material": draw_material(jax.random.fold_in(seeds[3], 71), 0),
        "source": gaussian(seeds[2], (NX, NY, NZ), 1.0, 6.0, ((0, 32),), jnp.float32),
    }


conductivity_table = (1.0, 0.72, 0.52, 0.37, 0.26, 0.18, 0.13, 0.09)
fine_step = 0.15
coarse_step = 0.3


def lookup(material):
    result = jnp.zeros(material.shape, jnp.float32)
    for number in range(8):
        result = jnp.where(material == number, jnp.float32(conductivity_table[number]), result)
    return result


def restrict(values):
    lead_dims = values.shape[:-3]
    folded = values.reshape(lead_dims + (values.shape[-3] // 2, 2, values.shape[-2] // 2, 2, values.shape[-1]))
    return jnp.mean(folded, axis=(-4, -2))


def prolong(values):
    lead_dims = values.shape[:-3]
    rows_x = values.shape[-3]
    rows_y = values.shape[-2]
    rows_z = values.shape[-1]
    spread = jnp.broadcast_to(values[..., :, None, :, None, :], lead_dims + (rows_x, 2, rows_y, 2, rows_z))
    return spread.reshape(lead_dims + (rows_x * 2, rows_y * 2, rows_z))


def make_faces(cond_pad, weight_x, weight_y, weight_z):
    own = cond_pad[1:-1]
    face_x = weight_x * 0.5 * (cond_pad[1:] + cond_pad[:-1])
    pad_y = jnp.pad(own, ((0, 0), (1, 1), (0, 0)))
    face_y = weight_y * 0.5 * (pad_y[:, 1:] + pad_y[:, :-1])
    pad_z = jnp.pad(own, ((0, 0), (0, 0), (1, 1)))
    face_z = weight_z * 0.5 * (pad_z[:, :, 1:] + pad_z[:, :, :-1])
    return face_x, face_y, face_z


def diffuse(padded, face_x, face_y, face_z, source_in, step_size):
    current = padded[1:-1]
    grad_x = face_x * (padded[1:] - padded[:-1])
    flux = grad_x[1:] - grad_x[:-1]
    field_y = jnp.pad(current, ((0, 0), (1, 1), (0, 0)))
    grad_y = face_y * (field_y[:, 1:] - field_y[:, :-1])
    flux = flux + grad_y[:, 1:] - grad_y[:, :-1]
    field_z = jnp.pad(current, ((0, 0), (0, 0), (1, 1)))
    grad_z = face_z * (field_z[:, :, 1:] - field_z[:, :, :-1])
    flux = flux + grad_z[:, :, 1:] - grad_z[:, :, :-1]
    return current + step_size * (flux + source_in)


def xpad(values):
    return jnp.pad(values, ((1, 1), (0, 0), (0, 0)))


def reference(starts, material, source):
    conduct = lookup(material)
    fine_faces = make_faces(xpad(conduct), 1.0, 1.0, 1.0)
    coarse_faces = make_faces(xpad(restrict(conduct)), 0.25, 0.25, 1.0)
    coarse_source = restrict(source)

    def fine_run(current):
        for step_num in range(FSTEPS):
            current = diffuse(xpad(current), fine_faces[0], fine_faces[1], fine_faces[2], source, fine_step)
        return current

    def coarse_run(current):
        reduced = restrict(current)
        for step_num in range(CSTEPS):
            reduced = diffuse(xpad(reduced), coarse_faces[0], coarse_faces[1], coarse_faces[2], coarse_source, coarse_step)
        return prolong(reduced)

    slabs = [starts[slab_num] for slab_num in range(N_TM)]
    coarse_now = [coarse_run(slab_start) for slab_start in slabs]
    offsets = []
    for iter_num in range(ITERS):
        offsets = [fine_run(slabs[slab_num]) - coarse_now[slab_num] for slab_num in range(N_TM)]
        updated = [slabs[0]]
        for slab_num in range(N_TM - 1):
            updated.append(coarse_run(updated[slab_num]) + offsets[slab_num])
        slabs = updated
        coarse_now = [coarse_run(slab_start) for slab_start in slabs]
    newest = coarse_now[-1] + offsets[-1]
    return jnp.stack([newest] + slabs[1:])
```

```python
import jax
import jax.numpy as jnp
from jax import lax
from jax.experimental import pallas as pl
from jax.experimental.pallas import tpu as pltpu
from jax.sharding import Mesh, PartitionSpec as P

SIZES = (4, 2, 8, 2, 2)
AXES = ("y", "l", "z", "h", "c")
SLABS = 8
ROWS = 8
NY = 256
NZ = 128
HALF = ROWS // 2
CY = NY // 2
PAD = 8
CHUNK = 64
FINE = 0.15
COARSE = 0.3
TABLE = (1.0, 0.72, 0.52, 0.37, 0.26, 0.18, 0.13, 0.09)

BLOCKS = 16
YB = CY // BLOCKS
YM = 16
YW = YB + 2 * YM
XH = 14
XW = 12 + 2 * XH
XALL = 16 + 2 * XH
KEEP = (8, 8, 6, 4, 4, 4, 2, 8)
STARTS = tuple(sum(KEEP[:i]) for i in range(len(KEEP)))
NKEEP = sum(KEEP)

EK, EU, E1, EKC, EUC, E1C, EDGE = 0, 256, 512, 768, 896, 1024, 1152

F32 = jnp.float32


def up_lane(x):
    return pltpu.roll(x, NZ - 1, axis=x.ndim - 1)


def down_lane(x):
    return pltpu.roll(x, 1, axis=x.ndim - 1)


def lanes(shape):
    return lax.broadcasted_iota(jnp.int32, shape, len(shape) - 1)


def lookup(material):
    result = jnp.zeros(material.shape, F32)
    for number in range(8):
        result = jnp.where(material == number, F32(TABLE[number]), result)
    return result


def z_faces(k, weight):
    lane = lanes(k.shape)
    upper = jnp.where(lane == NZ - 1, 0.0, up_lane(k))
    lower = jnp.where(lane == 0, 0.0, down_lane(k))
    above = weight * (k + upper)
    below = weight * (k + lower)
    return jnp.where(lane == NZ - 1, 0.0, above), above + below


def coefficients(kp, r, a, n, wx, wy, wz, below, above):
    k = kp[r, PAD + a : PAD + a + n]
    cyp = wy * (k + kp[r, PAD + a + 1 : PAD + a + n + 1])
    cym = wy * (k + kp[r, PAD + a - 1 : PAD + a + n - 1])
    cz, zsum = z_faces(k, wz)
    diag = 1.0 - (cyp + cym + zsum)
    cx = None
    if below:
        diag = diag - wx * (k + kp[r - 1, PAD + a : PAD + a + n])
    if above:
        cx = wx * (k + kp[r + 1, PAD + a : PAD + a + n])
        diag = diag - cx
    return cx, cyp, cym, cz, diag


def base(u, r, a, n, cx, cyp, cym, cz, diag, below, above):
    here = u[r, PAD + a : PAD + a + n]
    s = slice(a, a + n)
    new = diag[r, s] * here
    new = new + cyp[r, s] * u[r, PAD + a + 1 : PAD + a + n + 1]
    new = new + cym[r, s] * u[r, PAD + a - 1 : PAD + a + n - 1]
    c = cz[r, s]
    new = new + c * up_lane(here) + down_lane(c * here)
    if below:
        new = new + cx[r - 1, s] * u[r - 1, PAD + a : PAD + a + n]
    if above:
        new = new + cx[r, s] * u[r + 1, PAD + a : PAD + a + n]
    return new


def each_row(count, visit):
    visit(0, False, True)

    def body(r, carry):
        visit(r, True, True)
        return carry

    lax.fori_loop(1, count - 1, body, 0)
    visit(count - 1, True, False)


def pieces(width):
    return [(a, CHUNK) for a in range(0, width, CHUNK)]


def clear_margin(ref, width):
    rows = ref.shape[0]
    ref[:, 0:PAD] = jnp.zeros((rows, PAD, NZ), F32)
    ref[:, PAD + width : PAD + width + PAD] = jnp.zeros((rows, PAD, NZ), F32)


def halve(ref, x, margin):
    total = None
    for p in range(2):
        for q in range(2):
            part = ref[2 * x + p, pl.ds(margin + q, CY, 2), :]
            total = part if total is None else total + part
    return 0.25 * total


def first_kernel(pos, u_in, mat, src, sc, so, cx, cyp, cym, cz, dg, ccx, ccyp, ccym, ccz, cdg, kc_out, kp, up, kcp, ucp, edge):
    clear_margin(kp, NY)
    clear_margin(up, NY)
    clear_margin(kcp, CY)
    clear_margin(ucp, CY)

    def fill(r, carry):
        for a, n in pieces(NY):
            kp[r, PAD + a : PAD + a + n] = lookup(mat[r, a : a + n])
            up[r, PAD + a : PAD + a + n] = u_in[0, r, a : a + n]
        return carry

    lax.fori_loop(0, ROWS, fill, 0)
    for x in range(HALF):
        kcp[x, PAD : PAD + CY] = halve(kp, x, PAD)
        ucp[x, PAD : PAD + CY] = halve(up, x, PAD)
        kc_out[x] = kcp[x, PAD : PAD + CY]

    def fine(r, below, above):
        for a, n in pieces(NY):
            s = slice(a, a + n)
            fx, cyp[r, s], cym[r, s], cz[r, s], dg[r, s] = coefficients(kp, r, a, n, 0.5 * FINE, 0.5 * FINE, 0.5 * FINE, below, above)
            if above:
                cx[r, s] = fx

    each_row(ROWS, fine)

    def coarse(r, below, above):
        for a, n in pieces(CY):
            s = slice(a, a + n)
            fx, ccyp[r, s], ccym[r, s], ccz[r, s], cdg[r, s] = coefficients(
                kcp, r, a, n, 0.125 * COARSE, 0.125 * COARSE, 0.5 * COARSE, below, above
            )
            if above:
                ccx[r, s] = fx

    each_row(HALF, coarse)
    for side, r, x in ((0, 0, 0), (1, ROWS - 1, HALF - 1)):
        for a, n in pieces(NY):
            edge[side, EK + a : EK + a + n] = kp[r, PAD + a : PAD + a + n]
            edge[side, EU + a : EU + a + n] = up[r, PAD + a : PAD + a + n]
            edge[side, E1 + a : E1 + a + n] = base(up, r, a, n, cx, cyp, cym, cz, dg, side == 1, side == 0) + FINE * src[r, a : a + n]
        for a, n in pieces(CY):
            edge[side, EKC + a : EKC + a + n] = kcp[x, PAD + a : PAD + a + n]
            edge[side, EUC + a : EUC + a + n] = ucp[x, PAD + a : PAD + a + n]
            edge[side, E1C + a : E1C + a + n] = base(ucp, x, a, n, ccx, ccyp, ccym, ccz, cdg, side == 1, side == 0)
    c = pos[4]
    sc[...] = edge[1 - c]
    so[...] = edge[c]


def two_sweeps(a_ref, b_ref, halo, later, face, live, rows, width, coefs, source):
    def one(src_ref, dst_ref, planes):
        def visit(r, below, above):
            for a, n in pieces(width):
                new = base(src_ref, r, a, n, *coefs, below, above)
                if source is not None:
                    new = new + FINE * source[r, a : a + n]
                here = src_ref[r, PAD + a : PAD + a + n]
                if not below:
                    new = new + face(0, a, n) * (planes(0, a, n) - here)
                if not above:
                    new = new + face(1, a, n) * (planes(1, a, n) - here)
                dst_ref[r, PAD + a : PAD + a + n] = new

        each_row(rows, visit)

    def second(side, a, n):
        r = 0 if side == 0 else rows - 1
        flux = face(side, a, n) * (a_ref[r, PAD + a : PAD + a + n] - halo(side, a, n))
        return live[side] * (later(side, a, n) + flux)

    def kept(store):
        def write(side):
            for a, n in pieces(width):
                store[side, a : a + n] = second(side, a, n)

        return write

    return one, kept


def run_two(a_ref, b_ref, store, halo, later, face, live, rows, width, coefs, source):
    one, kept = two_sweeps(a_ref, b_ref, halo, later, face, live, rows, width, coefs, source)
    one(a_ref, b_ref, halo)
    kept(store)(0)
    kept(store)(1)
    one(b_ref, a_ref, lambda side, a, n: store[side, a : a + n])


def lives(pos):
    place = (pos[2] * 2 + pos[3]) * 2 + pos[4]
    return jnp.where(place > 0, F32(1), F32(0)), jnp.where(place < 31, F32(1), F32(0))


def second_kernel(
    pos, u_in, src, sc, so, rc, ro, cx, cyp, cym, cz, dg, ccx, ccyp, ccym, ccz, cdg,
    u_out, faces, au, tc, to, ua, ub, ca, cb, own, got, store, edge,
):
    c = pos[4]
    live = lives(pos)
    for ref in (ua, ub):
        clear_margin(ref, NY)
    for ref in (ca, cb):
        clear_margin(ref, CY)
    own[1 - c] = sc[...]
    own[c] = so[...]
    got[1 - c] = rc[...]
    got[c] = ro[...]
    for side in range(2):
        got[side] = got[side] * live[side]

    def fill(r, carry):
        for a, n in pieces(NY):
            ua[r, PAD + a : PAD + a + n] = u_in[0, r, a : a + n]
        return carry

    lax.fori_loop(0, ROWS, fill, 0)
    for x in range(HALF):
        ca[x, PAD : PAD + CY] = halve(ua, x, PAD)
    for side in range(2):
        for a, n in pieces(NY):
            faces[side, a : a + n] = (0.5 * FINE) * (own[side, EK + a : EK + a + n] + got[side, EK + a : EK + a + n])

    def plane(offset):
        return lambda side, a, n: got[side, offset + a : offset + a + n]

    def coarse_face(side, a, n):
        return (0.125 * COARSE) * (own[side, EKC + a : EKC + a + n] + got[side, EKC + a : EKC + a + n])

    run_two(
        ua, ub, store, plane(EU), plane(E1), lambda side, a, n: faces[side, a : a + n],
        live, ROWS, NY, (cx, cyp, cym, cz, dg), src,
    )
    for side, r in ((0, 0), (1, ROWS - 1)):
        for a, n in pieces(NY):
            edge[side, a : a + n] = ua[r, PAD + a : PAD + a + n]
            edge[side, NY + a : NY + a + n] = base(ua, r, a, n, cx, cyp, cym, cz, dg, side == 1, side == 0) + FINE * src[r, a : a + n]
    tc[...] = edge[1 - c]
    to[...] = edge[c]
    u_out[...] = ua[...]
    run_two(
        ca, cb, store, plane(EUC), plane(E1C), coarse_face,
        live, HALF, CY, (ccx, ccyp, ccym, ccz, cdg), None,
    )
    for x in range(HALF):
        au[x] = ca[x, PAD : PAD + CY]


def third_kernel(pos, u_in, src, faces, rc, ro, au, kc, cx, cyp, cym, cz, dg, h_out, strips, ua, ub, got, store, wp):
    c = pos[4]
    slab = pos[0] * 2 + pos[1]
    live = lives(pos)
    ua[...] = u_in[...]
    clear_margin(ub, NY)
    got[1 - c] = rc[...]
    got[c] = ro[...]
    for side in range(2):
        got[side] = got[side] * live[side]
    run_two(
        ua, ub, store,
        lambda side, a, n: got[side, a : a + n],
        lambda side, a, n: got[side, NY + a : NY + a + n],
        lambda side, a, n: faces[side, a : a + n],
        live, ROWS, NY, (cx, cyp, cym, cz, dg), src,
    )
    keep = jnp.where(slab > 0, F32(1), F32(0))
    wp[:, 0:YM] = jnp.zeros((HALF, YM, NZ), F32)
    wp[:, YM + CY : YM + CY + YM] = jnp.zeros((HALF, YM, NZ), F32)
    last = slab == SLABS - 1
    for x in range(HALF):
        coarse = keep * au[x]
        total = None
        for p in range(2):
            for q in range(2):
                part = ua[2 * x + p, pl.ds(PAD + q, CY, 2), :] - coarse
                h_out[2 * x + p, pl.ds(q, CY, 2), :] = part
                total = part if total is None else total + part
        wp[x, YM : YM + CY] = jnp.where(last, kc[x], 0.25 * total)
    for b in range(BLOCKS):
        strips[b] = wp[:, b * YB : b * YB + YW]


def pack_kernel(pos, own, even, odd):
    up = 1 - lax.rem(pos[2], 2)
    for j in range(SLABS):
        n = KEEP[j]
        even[STARTS[j] : STARTS[j] + n] = own[j, pl.ds(up * (8 - n), n)]
        odd[STARTS[j] : STARTS[j] + n] = own[j, pl.ds((1 - up) * (8 - n), n)]


def chain_kernel(pos, own, part, even, odd, peven, podd, out, w, ea, eb, cx, cyp, cym, cz, dg, kp):
    c = pos[4]
    z = pos[2]
    block = (pos[0] * 2 + pos[1]) * 2 + pos[3]
    is_up = 1 - lax.rem(z, 2)
    low = jnp.where(z > 0, F32(1), F32(0))
    high = jnp.where(z < 7, F32(1), F32(0))
    w[...] = jnp.zeros(w.shape, F32)
    for j in range(SLABS):
        for i in range(8):
            row = XH + 8 * (i // 4) + i % 4
            w[j, row + 4 * c] = own[j, i]
            w[j, row + 4 * (1 - c)] = part[j, i]
    for (e_ref, o_ref, core) in ((even, odd, c), (peven, podd, 1 - c)):
        for j in range(SLABS):
            n = KEEP[j]
            for t in range(n):
                i_low = 8 - n + t
                r_low = XH + 8 * (i_low // 4) + i_low % 4 - 16
                r_high = XH + 8 * (t // 4) + t % 4 + 16
                src = STARTS[j] + t
                from_even = e_ref[src]
                from_odd = o_ref[src]
                below = jnp.where(is_up == 1, from_odd, from_even) * low
                above = jnp.where(is_up == 1, from_even, from_odd) * high
                row = r_low + 4 * core

                @pl.when(row >= 0)
                def _():
                    w[j, jnp.maximum(row, 0)] = below

                row2 = r_high + 4 * core

                @pl.when(row2 < XALL)
                def _():
                    w[j, jnp.minimum(row2, XALL - 1)] = above

    first = 4 * c
    kp[...] = jnp.zeros(kp.shape, F32)
    ea[...] = jnp.zeros(ea.shape, F32)
    eb[...] = jnp.zeros(eb.shape, F32)
    ycell = block * YB - YM + lax.broadcasted_iota(jnp.int32, (YW, NZ), 0)
    ymask = jnp.where((ycell >= 0) & (ycell < CY), F32(1), F32(0))

    def fill(r, carry):
        kp[r, PAD : PAD + YW] = w[7, first + r]
        ea[r, PAD : PAD + YW] = w[0, first + r]
        return carry

    lax.fori_loop(0, XW, fill, 0)
    wx = 0.125 * COARSE
    wz = 0.5 * COARSE

    def coef(r, carry):
        k = kp[r, PAD : PAD + YW]
        kup = kp[r + 1, PAD : PAD + YW]
        kdn = kp[jnp.maximum(r - 1, 0), PAD : PAD + YW]
        a = wx * (k + kp[r, PAD + 1 : PAD + YW + 1])
        b = wx * (k + kp[r, PAD - 1 : PAD + YW - 1])
        zc, zsum = z_faces(k, wz)
        above = wx * (k + kup)
        below = wx * (k + kdn)
        row = 16 * z + 4 * c - XH + r
        inside = jnp.where((row >= 0) & (row < CY), F32(1), F32(0))
        m = ymask * inside
        cyp[r] = a * m
        cym[r] = b * m
        cz[r] = zc * m
        cx[r, 0] = below * m
        cx[r, 1] = above * m
        dg[r] = (1.0 - (a + b + zsum + above + below)) * m
        return carry

    lax.fori_loop(0, XW, coef, 0)

    def sweep(src, dst, lo, hi, add=None):
        def body(r, carry):
            here = src[r, PAD : PAD + YW]
            new = dg[r] * here
            new = new + cyp[r] * src[r, PAD + 1 : PAD + YW + 1]
            new = new + cym[r] * src[r, PAD - 1 : PAD + YW - 1]
            zc = cz[r]
            new = new + zc * up_lane(here) + down_lane(zc * here)
            new = new + cx[r, 0] * src[r - 1, PAD : PAD + YW]
            new = new + cx[r, 1] * src[r + 1, PAD : PAD + YW]
            dst[r, PAD : PAD + YW] = new
            return carry

        lax.fori_loop(lo, hi, body, 0)

    out[2:4] = jnp.zeros((2, HALF, YB, NZ), F32)
    for k in range(1, 8):
        done = 2 * (k - 1)
        sweep(ea, eb, done + 1, XW - done - 1)
        sweep(eb, ea, done + 2, XW - done - 2)
        m = (k + 1) % SLABS
        for side in range(2):
            for i in range(HALF):
                out[2 * m + side, i] = ea[XH + 8 * side + i, PAD + YM : PAD + YM + YB]
        if k < 7:
            def add(r, carry):
                ea[r, PAD : PAD + YW] = ea[r, PAD : PAD + YW] + w[k, first + r]
                return carry

            lax.fori_loop(done + 2, XW - done - 2, add, 0)


def last_kernel(h_in, y_in, out):
    for x in range(HALF):
        fix = y_in[:, x].reshape(CY, NZ)
        for p in range(2):
            for q in range(2):
                out[0, 2 * x + p, pl.ds(q, CY, 2), :] = h_in[2 * x + p, pl.ds(q, CY, 2), :] + fix


def shape(*dims):
    return jax.ShapeDtypeStruct(dims, F32)


def call(kernel, outs, scratch, count, with_pos=True):
    vmem = pl.BlockSpec(memory_space=pltpu.VMEM)
    smem = pl.BlockSpec(memory_space=pltpu.SMEM)
    return pl.pallas_call(
        kernel,
        out_shape=outs,
        in_specs=([smem] if with_pos else []) + [vmem] * count,
        out_specs=jax.tree.map(lambda _: vmem, outs),
        scratch_shapes=[pltpu.VMEM(s, F32) for s in scratch],
    )


def pairs(n, odd):
    found = []
    for i in range(odd, n - 1, 2):
        found += [(i, i + 1), (i + 1, i)]
    if odd:
        found += [(0, n - 1), (n - 1, 0)]
    return found


SPACE = ("z", "h", "c")
PLANE = ("y", "l", "h")


def local(starts, material, source):
    pos = jnp.stack([lax.axis_index(a) for a in AXES]).astype(jnp.int32)
    fine = shape(ROWS, NY, NZ)
    crs = shape(HALF, CY, NZ)
    padded = (ROWS, NY + 2 * PAD, NZ)
    cpad = (HALF, CY + 2 * PAD, NZ)

    def swap_c(x):
        return lax.ppermute(x, "c", pairs(2, 0))

    def swap_o(x):
        return lax.ppermute(x, SPACE, pairs(32, 1))

    sc, so, cx, cyp, cym, cz, dg, ccx, ccyp, ccym, ccz, cdg, kc = call(
        first_kernel,
        (shape(EDGE, NZ), shape(EDGE, NZ), fine, fine, fine, fine, fine, crs, crs, crs, crs, crs, crs),
        (padded, padded, cpad, cpad, (2, EDGE, NZ)),
        3,
    )(pos, starts, material, source)
    ro = swap_o(so)
    rc = swap_c(sc)
    u2, faces, au, tc, to = call(
        second_kernel,
        (shape(*padded), shape(2, NY, NZ), crs, shape(2 * NY, NZ), shape(2 * NY, NZ)),
        (padded, padded, cpad, cpad, (2, EDGE, NZ), (2, EDGE, NZ), (2, NY, NZ), (2, 2 * NY, NZ)),
        16,
    )(pos, starts, source, sc, so, rc, ro, cx, cyp, cym, cz, dg, ccx, ccyp, ccym, ccz, cdg)
    ro2 = swap_o(to)
    rc2 = swap_c(tc)
    moved, strips = call(
        third_kernel,
        (fine, shape(BLOCKS, HALF, YW, NZ)),
        (padded, padded, (2, 2 * NY, NZ), (2, NY, NZ), (HALF, CY + 2 * YM, NZ)),
        12,
    )(pos, u2, source, faces, rc2, ro2, au, kc, cx, cyp, cym, cz, dg)
    own = lax.all_to_all(strips, PLANE, 0, 0, tiled=True)
    own, moved = lax.optimization_barrier((own, moved))
    own = own.reshape(SLABS, 8, YW, NZ)
    even, odd = call(pack_kernel, (shape(NKEEP, YW, NZ), shape(NKEEP, YW, NZ)), (), 1)(pos, own)
    moved = lax.ppermute(moved, ("y", "l"), [(i, (i + 1) % 8) for i in range(8)])
    even = lax.ppermute(even, "z", pairs(8, 0))
    odd = lax.ppermute(odd, "z", pairs(8, 1))
    part = swap_c(own)
    peven = swap_c(even)
    podd = swap_c(odd)
    dom = (XW + 1, YW + 2 * PAD, NZ)
    (fixes,) = call(
        chain_kernel,
        (shape(BLOCKS, HALF, YB, NZ),),
        (
            (SLABS, XALL, YW, NZ), dom, dom, (XW, 2, YW, NZ), (XW, YW, NZ), (XW, YW, NZ), (XW, YW, NZ), (XW, YW, NZ), dom,
        ),
        6,
    )(pos, own, part, even, odd, peven, podd)
    fixes = lax.all_to_all(fixes, PLANE, 0, 0, tiled=True)
    (result,) = call(last_kernel, (shape(1, ROWS, NY, NZ),), (), 2, with_pos=False)(moved, fixes)
    return result


def solution(mesh):
    refined = Mesh(mesh.devices.reshape(SIZES), AXES)
    in_specs = (P(("y", "l"), SPACE, None, None), P(SPACE, None, None), P(SPACE, None, None))
    out_specs = P(("y", "l"), SPACE, None, None)
    return jax.shard_map(local, mesh=refined, in_specs=in_specs, out_specs=out_specs, check_vma=False)
```

```python
import jax
import jax.numpy as jnp
from jax import lax
from jax.experimental import pallas as pl
from jax.experimental.pallas import tpu as pltpu
from jax.sharding import Mesh, PartitionSpec as P

SIZES = (4, 2, 8, 2, 2)
AXES = ("y", "l", "z", "h", "c")
SLABS = 8
ROWS = 8
NY = 256
NZ = 128
HALF = ROWS // 2
CY = NY // 2
PAD = 8
CHUNK = 64
FINE = 0.15
COARSE = 0.3
TABLE = (1.0, 0.72, 0.52, 0.37, 0.26, 0.18, 0.13, 0.09)

BLOCKS = 16
YB = CY // BLOCKS
YM = 16
YW = YB + 2 * YM
XH = 14
XW = 12 + 2 * XH
XALL = 48
KEEP = (8, 8, 6, 4, 4, 4, 2)
YCUT = (0, 0, 0, 8, 8, 8, 8)
WIDE = tuple(YW - 2 * cut for cut in YCUT)
STARTS = tuple(sum(KEEP[i] * WIDE[i] for i in range(j)) for j in range(8))
NSEND = STARTS[7]

EK, EU, E1, EKC, EUC, E1C, EDGE = 0, 256, 512, 768, 896, 1024, 1152

F32 = jnp.float32


def up_lane(x):
    return pltpu.roll(x, NZ - 1, axis=x.ndim - 1)


def down_lane(x):
    return pltpu.roll(x, 1, axis=x.ndim - 1)


def lanes(shape):
    return lax.broadcasted_iota(jnp.int32, shape, len(shape) - 1)


def lookup(material):
    result = jnp.zeros(material.shape, F32)
    for number in range(8):
        result = jnp.where(material == number, F32(TABLE[number]), result)
    return result


def z_faces(k, weight):
    lane = lanes(k.shape)
    upper = jnp.where(lane == NZ - 1, 0.0, up_lane(k))
    lower = jnp.where(lane == 0, 0.0, down_lane(k))
    above = weight * (k + upper)
    below = weight * (k + lower)
    return jnp.where(lane == NZ - 1, 0.0, above), above + below


def coefficients(kp, r, a, n, wx, wy, wz, below, above):
    k = kp[r, PAD + a : PAD + a + n]
    cyp = wy * (k + kp[r, PAD + a + 1 : PAD + a + n + 1])
    cym = wy * (k + kp[r, PAD + a - 1 : PAD + a + n - 1])
    cz, zsum = z_faces(k, wz)
    diag = 1.0 - (cyp + cym + zsum)
    cx = None
    if below:
        diag = diag - wx * (k + kp[r - 1, PAD + a : PAD + a + n])
    if above:
        cx = wx * (k + kp[r + 1, PAD + a : PAD + a + n])
        diag = diag - cx
    return cx, cyp, cym, cz, diag


def combine(u, r, a, n, cx_below, cx_above, cyp, cym, cz, diag):
    here = u[r, PAD + a : PAD + a + n]
    new = diag * here
    new = new + cyp * u[r, PAD + a + 1 : PAD + a + n + 1]
    new = new + cym * u[r, PAD + a - 1 : PAD + a + n - 1]
    new = new + cz * up_lane(here) + down_lane(cz * here)
    if cx_below is not None:
        new = new + cx_below * u[r - 1, PAD + a : PAD + a + n]
    if cx_above is not None:
        new = new + cx_above * u[r + 1, PAD + a : PAD + a + n]
    return new


def base(u, r, a, n, cx, cyp, cym, cz, diag, below, above):
    s = slice(a, a + n)
    return combine(
        u, r, a, n, cx[r - 1, s] if below else None, cx[r, s] if above else None, cyp[r, s], cym[r, s], cz[r, s], diag[r, s]
    )


def edge_sweep(kp, u, side, rows, a, n, wx, wy, wz):
    r = 0 if side == 0 else rows - 1
    cx, cyp, cym, cz, diag = coefficients(kp, r, a, n, wx, wy, wz, side == 1, side == 0)
    below = wx * (kp[r, PAD + a : PAD + a + n] + kp[r - 1, PAD + a : PAD + a + n]) if side == 1 else None
    return combine(u, r, a, n, below, cx, cyp, cym, cz, diag)


def each_row(count, visit):
    visit(0, False, True)

    def body(r, carry):
        visit(r, True, True)
        return carry

    lax.fori_loop(1, count - 1, body, 0)
    visit(count - 1, True, False)


def pieces(width):
    return [(a, CHUNK) for a in range(0, width, CHUNK)]


def clear_margin(ref, width):
    rows = ref.shape[0]
    ref[:, 0:PAD] = jnp.zeros((rows, PAD, NZ), F32)
    ref[:, PAD + width : PAD + width + PAD] = jnp.zeros((rows, PAD, NZ), F32)


def halve(ref, x, margin):
    total = None
    for p in range(2):
        for q in range(2):
            part = ref[2 * x + p, pl.ds(margin + q, CY, 2), :]
            total = part if total is None else total + part
    return 0.25 * total


FINE_W = (0.5 * FINE, 0.5 * FINE, 0.5 * FINE)
COARSE_W = (0.125 * COARSE, 0.125 * COARSE, 0.5 * COARSE)


def place(name):
    return lax.axis_index(name)


def block_of(h):
    return (place("y") * 2 + place("l")) * 2 + h


def lives():
    index = (place("z") * 2 + place("h")) * 2 + place("c")
    return jnp.where(index > 0, F32(1), F32(0)), jnp.where(index < 31, F32(1), F32(0))


def first_kernel(u_in, mat, src, sc, so, kp, up, kcp, ucp, edge, numbers, ends, u_sem, m_sem, s_sem):
    inside = pl.ds(PAD, NY)
    order = (0, 7, 1, 6, 2, 5, 3, 4)
    for side, r in ((0, 0), (1, ROWS - 1)):
        pltpu.make_async_copy(src.at[r], ends.at[side], s_sem.at[side]).start()
    for r in order:
        pltpu.make_async_copy(mat.at[r], numbers.at[r], m_sem.at[r]).start()
        pltpu.make_async_copy(u_in.at[0, r], up.at[r, inside], u_sem.at[r]).start()
    clear_margin(kp, NY)
    clear_margin(up, NY)
    clear_margin(kcp, CY)
    clear_margin(ucp, CY)
    for r in order:
        pltpu.make_async_copy(mat.at[r], numbers.at[r], m_sem.at[r]).wait()
        for a, n in pieces(NY):
            kp[r, PAD + a : PAD + a + n] = lookup(numbers[r, a : a + n])
    for r in range(ROWS):
        pltpu.make_async_copy(u_in.at[0, r], up.at[r, inside], u_sem.at[r]).wait()
    for side, r in ((0, 0), (1, ROWS - 1)):
        pltpu.make_async_copy(src.at[r], ends.at[side], s_sem.at[side]).wait()
    for x in range(HALF):
        kcp[x, PAD : PAD + CY] = halve(kp, x, PAD)
        ucp[x, PAD : PAD + CY] = halve(up, x, PAD)
    for side, r, x in ((0, 0, 0), (1, ROWS - 1, HALF - 1)):
        for a, n in pieces(NY):
            edge[side, EK + a : EK + a + n] = kp[r, PAD + a : PAD + a + n]
            edge[side, EU + a : EU + a + n] = up[r, PAD + a : PAD + a + n]
            edge[side, E1 + a : E1 + a + n] = edge_sweep(kp, up, side, ROWS, a, n, *FINE_W) + FINE * ends[side, a : a + n]
        for a, n in pieces(CY):
            edge[side, EKC + a : EKC + a + n] = kcp[x, PAD + a : PAD + a + n]
            edge[side, EUC + a : EUC + a + n] = ucp[x, PAD + a : PAD + a + n]
            edge[side, E1C + a : E1C + a + n] = edge_sweep(kcp, ucp, side, HALF, a, n, *COARSE_W)
    c = place("c")
    sc[...] = edge[1 - c]
    so[...] = edge[c]


def coef_kernel(kp, up, src, kcp, ucp, cx, cyp, cym, cz, dg, ccx, ccyp, ccym, ccz, cdg, b1, cb1, strip, strip_h, kw):
    clear_margin(b1, NY)
    clear_margin(cb1, CY)
    kw[:, 0:YM] = jnp.zeros((HALF, YM, NZ), F32)
    kw[:, YM + CY : YM + CY + YM] = jnp.zeros((HALF, YM, NZ), F32)
    kw[:, YM : YM + CY] = kcp[:, PAD : PAD + CY]
    h = place("h")
    strip[...] = kw[:, pl.ds(pl.multiple_of(block_of(h) * YB, 8), YW)]
    strip_h[...] = kw[:, pl.ds(pl.multiple_of(block_of(1 - h) * YB, 8), YW)]

    def make(k, u, n_all, weights, outs, target, source):
        fx, fyp, fym, fz, fd = outs

        def visit(r, below, above):
            for a, n in pieces(n_all):
                s = slice(a, a + n)
                wx = weights[0]
                above_c, yp, ym, zc, dd = coefficients(k, r, a, n, *weights, below, above)
                fyp[r, s], fym[r, s], fz[r, s], fd[r, s] = yp, ym, zc, dd
                if above:
                    fx[r, s] = above_c
                under = wx * (k[r, PAD + a : PAD + a + n] + k[r - 1, PAD + a : PAD + a + n]) if below else None
                new = combine(u, r, a, n, under, above_c, yp, ym, zc, dd)
                if source is not None:
                    new = new + FINE * source[r, s]
                target[r, PAD + a : PAD + a + n] = new

        each_row(u.shape[0], visit)

    make(kp, up, NY, FINE_W, (cx, cyp, cym, cz, dg), b1, src)
    make(kcp, ucp, CY, COARSE_W, (ccx, ccyp, ccym, ccz, cdg), cb1, None)


def fix_rows(target, old, swept, halo, face, rows, width):
    target[...] = swept[...]
    for side, r in ((0, 0), (1, rows - 1)):
        for a, n in pieces(width):
            s = slice(PAD + a, PAD + a + n)
            target[r, s] = swept[r, s] + face(side, a, n) * (halo(side, a, n) - old[r, s])


def halo_after(store, old, halo, later, face, live, rows, width):
    for side, r in ((0, 0), (1, rows - 1)):
        for a, n in pieces(width):
            flux = face(side, a, n) * (old[r, PAD + a : PAD + a + n] - halo(side, a, n))
            store[side, a : a + n] = live[side] * (later(side, a, n) + flux)


def full_sweep(dst, src_ref, store, face, rows, width, coefs, source):
    def visit(r, below, above):
        for a, n in pieces(width):
            new = base(src_ref, r, a, n, *coefs, below, above)
            if source is not None:
                new = new + FINE * source[r, a : a + n]
            here = src_ref[r, PAD + a : PAD + a + n]
            if not below:
                new = new + face(0, a, n) * (store[0, a : a + n] - here)
            if not above:
                new = new + face(1, a, n) * (store[1, a : a + n] - here)
            dst[r, PAD + a : PAD + a + n] = new

    each_row(rows, visit)


def reader(ref, offset=0):
    return lambda side, a, n: ref[side, offset + a : offset + a + n]


def second_kernel(
    src, sc, so, rc, ro, up, ucp, b1, cb1, strip, strip_h, cx, cyp, cym, cz, dg, u2, faces, c1, cfaces, cstore, tc, to, kown, own, got, store, edge, u1,
):
    c = place("c")
    h = place("h")
    kown[pl.ds(4 * h, HALF)] = strip[...]
    kown[pl.ds(4 * (1 - h), HALF)] = strip_h[...]
    live = lives()
    own[1 - c] = sc[...]
    own[c] = so[...]
    got[1 - c] = rc[...]
    got[c] = ro[...]
    for side in range(2):
        got[side] = got[side] * live[side]
        for a, n in pieces(NY):
            faces[side, a : a + n] = (0.5 * FINE) * (own[side, EK + a : EK + a + n] + got[side, EK + a : EK + a + n])
        for a, n in pieces(CY):
            cfaces[side, a : a + n] = (0.125 * COARSE) * (own[side, EKC + a : EKC + a + n] + got[side, EKC + a : EKC + a + n])
    clear_margin(u2, NY)
    halo_after(store, up, reader(got, EU), reader(got, E1), reader(faces), live, ROWS, NY)
    fix_rows(u1, up, b1, reader(got, EU), reader(faces), ROWS, NY)
    coefs = (cx, cyp, cym, cz, dg)
    full_sweep(u2, u1, store, reader(faces), ROWS, NY, coefs, src)
    for side, r in ((0, 0), (1, ROWS - 1)):
        for a, n in pieces(NY):
            edge[side, a : a + n] = u2[r, PAD + a : PAD + a + n]
            edge[side, NY + a : NY + a + n] = base(u2, r, a, n, *coefs, side == 1, side == 0) + FINE * src[r, a : a + n]
    tc[...] = edge[1 - c]
    to[...] = edge[c]
    halo_after(cstore, ucp, reader(got, EUC), reader(got, E1C), reader(cfaces), live, HALF, CY)
    fix_rows(c1, ucp, cb1, reader(got, EUC), reader(cfaces), HALF, CY)


def middle_kernel(u2, src, c1, cstore, cfaces, cx, cyp, cym, cz, dg, ccx, ccyp, ccym, ccz, cdg, b3, au):
    clear_margin(b3, NY)
    clear_margin(au, CY)

    def visit(r, below, above):
        for a, n in pieces(NY):
            b3[r, PAD + a : PAD + a + n] = base(u2, r, a, n, cx, cyp, cym, cz, dg, below, above) + FINE * src[r, a : a + n]

    each_row(ROWS, visit)
    full_sweep(au, c1, cstore, reader(cfaces), HALF, CY, (ccx, ccyp, ccym, ccz, cdg), None)


def third_kernel(
    u2, src, faces, rc, ro, b3, au, kown, keven, kodd, cx, cyp, cym, cz, dg, h_out, strips, kall, got, store, u3, f, wp,
):
    kall[0:8] = kown[...]
    kall[8:16] = keven[...]
    kall[16:24] = kodd[...]
    c = place("c")
    live = lives()
    got[1 - c] = rc[...]
    got[c] = ro[...]
    for side in range(2):
        got[side] = got[side] * live[side]
    halo_after(store, u2, reader(got), reader(got, NY), reader(faces), live, ROWS, NY)
    fix_rows(u3, u2, b3, reader(got), reader(faces), ROWS, NY)
    full_sweep(f, u3, store, reader(faces), ROWS, NY, (cx, cyp, cym, cz, dg), src)
    keep = jnp.where(place("y") + place("l") > 0, F32(1), F32(0))
    wp[:, 0:YM] = jnp.zeros((HALF, YM, NZ), F32)
    wp[:, YM + CY : YM + CY + YM] = jnp.zeros((HALF, YM, NZ), F32)
    for x in range(HALF):
        coarse = keep * au[x, PAD : PAD + CY]
        total = None
        for p in range(2):
            for q in range(2):
                part = f[2 * x + p, pl.ds(PAD + q, CY, 2), :] - coarse
                h_out[2 * x + p, pl.ds(q, CY, 2), :] = part
                total = part if total is None else total + part
        wp[x, YM : YM + CY] = 0.25 * total
    for b in range(BLOCKS):
        strips[b] = wp[:, b * YB : b * YB + YW]


def pack_kernel(own, even, odd):
    up = 1 - lax.rem(place("z"), 2)
    for j in range(7):
        n, cut, wide = KEEP[j], YCUT[j], WIDE[j]
        for t in range(n):
            at = STARTS[j] + t * wide
            even[at : at + wide] = own[j, up * (8 - n) + t, cut : cut + wide]
            odd[at : at + wide] = own[j, (1 - up) * (8 - n) + t, cut : cut + wide]


def position(i):
    return 8 * (i // 4) + i % 4


def patch_kernel(kall, pkall, cxp, cyp, cym, cz, dg, kp):
    c = place("c")
    z = place("z")
    is_up = 1 - lax.rem(z, 2)
    low = jnp.where(z > 0, F32(1), F32(0))
    high = jnp.where(z < 7, F32(1), F32(0))
    first = 4 * c + 16 - XH
    kp[:, 0:PAD] = jnp.zeros((XALL, PAD, NZ), F32)
    kp[:, PAD + YW : PAD + YW + PAD] = jnp.zeros((XALL, PAD, NZ), F32)
    for core, k_ref in ((c, kall), (1 - c, pkall)):
        shift = 16 + 4 * core
        for i in range(8):
            kp[shift + position(i), PAD : PAD + YW] = k_ref[i]

            kp[shift + position(i) - 16, PAD : PAD + YW] = k_ref[8 * (1 + is_up) + i] * low
            kp[shift + position(i) + 16, PAD : PAD + YW] = k_ref[8 * (2 - is_up) + i] * high

    ycell = block_of(place("h")) * YB - YM + lax.broadcasted_iota(jnp.int32, (YW, NZ), 0)
    ymask = jnp.where((ycell >= 0) & (ycell < CY), F32(1), F32(0))
    wx, _, wz = COARSE_W

    def coef(g, carry):
        for t in range(4):
            r = 4 * g + t
            q = first + r
            k = kp[q, PAD : PAD + YW]
            a = wx * (k + kp[q, PAD + 1 : PAD + YW + 1])
            b = wx * (k + kp[q, PAD - 1 : PAD + YW - 1])
            zc, zsum = z_faces(k, wz)
            above = wx * (k + kp[q + 1, PAD : PAD + YW])
            below = wx * (k + kp[q - 1, PAD : PAD + YW])
            row = 16 * z + 4 * c - XH + r
            m = ymask * jnp.where((row >= 0) & (row < CY), F32(1), F32(0))
            m_above = ymask * jnp.where((row >= 0) & (row < CY - 1), F32(1), F32(0))
            cyp[r] = a * m
            cym[r] = b * m
            cz[r] = zc * m
            cxp[r] = above * m_above
            dg[r] = (1.0 - (a + b + zsum + above + below)) * m
        return carry

    lax.fori_loop(0, XW // 4, coef, 0)


def chain_kernel(own, part, even, odd, peven, podd, cxp, cyp, cym, cz, dg, out, w, ea, eb):
    c = place("c")
    z = place("z")
    is_up = lax.rem(z, 2) == 0
    low = jnp.where(z > 0, F32(1), F32(0))
    high = jnp.where(z < 7, F32(1), F32(0))
    first = 4 * c + 16 - XH

    for core, mine, e_ref, o_ref in ((c, own, even, odd), (1 - c, part, peven, podd)):
        shift = 16 + 4 * core
        for j in range(7):
            for i in range(8):
                w[j, shift + position(i)] = mine[j, i]

        def fill(from_below, from_above):
            for j in range(7):
                n, cut, wide = KEEP[j], YCUT[j], WIDE[j]
                for t in range(n):
                    at = STARTS[j] + t * wide
                    w[j, shift + position(8 - n + t) - 16, cut : cut + wide] = from_below[at : at + wide] * low
                    w[j, shift + position(t) + 16, cut : cut + wide] = from_above[at : at + wide] * high

        @pl.when(is_up)
        def _():
            fill(o_ref, e_ref)

        @pl.when(jnp.logical_not(is_up))
        def _():
            fill(e_ref, o_ref)

    for r in range(XW):
        ea[r, PAD : PAD + YW] = w[0, first + r]

    def halved(lo, hi, visit):
        half = (hi - lo) // 2

        def body(g, carry):
            for t in range(half):
                visit(lo + g * half + t)
            return carry

        lax.fori_loop(0, 2, body, 0)

    def sweep(src, dst, number, added):
        cut = 0 if number <= 5 else 8
        s = slice(cut, YW - cut)
        n = YW - 2 * cut

        def visit(r):
            here = src[r, PAD + cut : PAD + cut + n]
            zc = cz[r, s]
            new = dg[r, s] * here + cyp[r, s] * src[r, PAD + cut + 1 : PAD + cut + n + 1]
            new = new + cym[r, s] * src[r, PAD + cut - 1 : PAD + cut + n - 1]
            new = new + (cxp[r - 1, s] * src[r - 1, PAD + cut : PAD + cut + n] + cxp[r, s] * src[r + 1, PAD + cut : PAD + cut + n])
            dst[r, PAD + cut : PAD + cut + n] = new + (zc * up_lane(here) + down_lane(zc * here))

        halved(number, XW - number, visit)

    out[2:4] = jnp.zeros((2, HALF, YB, NZ), F32)
    for k in range(1, 8):
        sweep(ea, eb, 2 * k - 1, None)
        sweep(eb, ea, 2 * k, None)
        m = (k + 1) % SLABS
        for side in range(2):
            for i in range(HALF):
                out[2 * m + side, i] = ea[XH + 8 * side + i, PAD + YM : PAD + YM + YB]
        if k < 7:
            cut = YCUT[k]
            s = slice(PAD + cut, PAD + YW - cut)

            def add(r):
                ea[r, s] = ea[r, s] + w[k, first + r, cut : YW - cut]

            halved(2 * k, XW - 2 * k, add)


def last_kernel(h_in, y_in, out):
    for x in range(HALF):
        fix = y_in[:, x].reshape(CY, NZ)
        for p in range(2):
            for q in range(2):
                out[0, 2 * x + p, pl.ds(q, CY, 2), :] = h_in[2 * x + p, pl.ds(q, CY, 2), :] + fix


def call(kernel, outs, scratch, *operands, limit=10, specs=None):
    vmem = pl.BlockSpec(memory_space=pltpu.VMEM)
    return pl.pallas_call(
        kernel,
        out_shape=[jax.ShapeDtypeStruct(s, F32) for s in outs],
        in_specs=specs or [vmem] * len(operands),
        out_specs=[vmem] * len(outs),
        scratch_shapes=[s if callable(getattr(s, "get_ref_aval", None)) else pltpu.VMEM(s, F32) for s in scratch],
        compiler_params=pltpu.CompilerParams(vmem_limit_bytes=limit * 1024 * 1024),
    )(*operands)


def pairs(n, odd):
    found = []
    for i in range(odd, n - 1, 2):
        found += [(i, i + 1), (i + 1, i)]
    if odd:
        found += [(0, n - 1), (n - 1, 0)]
    return found


SPACE = ("z", "h", "c")
PLANE = ("y", "l", "h")


def local(starts, material, source):
    fine = (ROWS, NY, NZ)
    crs = (HALF, CY, NZ)
    padded = (ROWS, NY + 2 * PAD, NZ)
    cpad = (HALF, CY + 2 * PAD, NZ)
    strip_shape = (HALF, YW, NZ)

    def swap_c(x):
        return lax.ppermute(x, "c", pairs(2, 0))

    def swap_o(x):
        return lax.ppermute(x, SPACE, pairs(32, 1))

    dma = pltpu.SemaphoreType.DMA
    sc, so, kp, up, kcp, ucp = call(
        first_kernel,
        ((EDGE, NZ), (EDGE, NZ), padded, padded, cpad, cpad),
        ((2, EDGE, NZ), pltpu.VMEM(fine, jnp.int32), (2, NY, NZ), dma((ROWS,)), dma((ROWS,)), dma((2,))),
        *(pltpu.with_memory_space_constraint(x, pltpu.HBM) for x in (starts, material, source)),
        specs=[pl.BlockSpec(memory_space=pltpu.HBM)] * 3,
    )
    rc = swap_c(sc)
    ro = swap_o(so)
    *coefs, b1, cb1, strip, strip_h = call(
        coef_kernel, (fine,) * 5 + (crs,) * 5 + (padded, cpad, strip_shape, strip_shape), ((HALF, CY + 2 * YM, NZ),),
        kp, up, source, kcp, ucp,
    )
    strip_h = lax.ppermute(strip_h, "h", pairs(2, 0))
    u2, faces, c1, cfaces, cstore, tc, to, kown = call(
        second_kernel,
        (padded, (2, NY, NZ), cpad, (2, CY, NZ), (2, CY, NZ), (2 * NY, NZ), (2 * NY, NZ), (8, YW, NZ)),
        ((2, EDGE, NZ), (2, EDGE, NZ), (2, NY, NZ), (2, 2 * NY, NZ), padded),
        source, sc, so, rc, ro, up, ucp, b1, cb1, strip, strip_h, *coefs[:5],
    )
    rc2 = swap_c(tc)
    ro2 = swap_o(to)
    keven = lax.ppermute(kown, "z", pairs(8, 0))
    kodd = lax.ppermute(kown, "z", pairs(8, 1))
    b3, au = call(middle_kernel, (padded, cpad), (), u2, source, c1, cstore, cfaces, *coefs)
    moved, strips, kall = call(
        third_kernel,
        (fine, (BLOCKS, HALF, YW, NZ), (24, YW, NZ)),
        ((2, 2 * NY, NZ), (2, NY, NZ), padded, padded, (HALF, CY + 2 * YM, NZ)),
        u2, source, faces, rc2, ro2, b3, au, kown, keven, kodd, *coefs[:5],
    )
    own = lax.all_to_all(strips, PLANE, 0, 0, tiled=True)
    own, moved = lax.optimization_barrier((own, moved))
    own = own.reshape(SLABS, 8, YW, NZ)
    even, odd = call(pack_kernel, ((NSEND, NZ), (NSEND, NZ)), (), own)
    even = lax.ppermute(even, "z", pairs(8, 0))
    odd = lax.ppermute(odd, "z", pairs(8, 1))
    part = swap_c(own)
    moved = lax.ppermute(moved, ("y", "l"), [(i, (i + 1) % 8) for i in range(8)])
    peven = swap_c(even)
    podd = swap_c(odd)
    dom = (XW + 1, YW + 2 * PAD, NZ)
    flat = (XW, YW, NZ)
    patch = call(patch_kernel, (flat,) * 5, ((XALL, YW + 2 * PAD, NZ),), kall, swap_c(kall))
    (fixes,) = call(
        chain_kernel, ((BLOCKS, HALF, YB, NZ),), ((7, XALL, YW, NZ), dom, dom),
        own, part, even, odd, peven, podd, *patch, limit=18,
    )
    fixes = lax.all_to_all(fixes, PLANE, 0, 0, tiled=True)
    (result,) = call(last_kernel, ((1, ROWS, NY, NZ),), (), moved, fixes)
    return result


def solution(mesh):
    refined = Mesh(mesh.devices.reshape(SIZES), AXES)
    in_specs = (P(("y", "l"), SPACE, None, None), P(SPACE, None, None), P(SPACE, None, None))
    out_specs = P(("y", "l"), SPACE, None, None)
    return jax.shard_map(local, mesh=refined, in_specs=in_specs, out_specs=out_specs, check_vma=False)
```

```python
import jax
import jax.numpy as jnp
from jax import lax
from jax.experimental import pallas as pl
from jax.experimental.pallas import tpu as pltpu
from jax.sharding import Mesh, PartitionSpec as P


SIZES = (4, 2, 8, 2, 2)
AXES = ("y", "l", "z", "h", "c")
SLABS = 8
ROWS = 8
NY = 256
NZ = 128
HALF = ROWS // 2
CY = NY // 2
PAD = 8
CHUNK = 64
FINE = 0.15
COARSE = 0.3
TABLE = (1.0, 0.72, 0.52, 0.37, 0.26, 0.18, 0.13, 0.09)

BLOCKS = 16
YB = CY // BLOCKS
YM = 14
WM = 16
YW = YB + 2 * YM
XH = 14
XW = 12 + 2 * XH
XALL = 48
KEEP = (8, 8, 6, 4, 4, 4, 2)
YCUT = (0, 2, 4, 6, 8, 10, 12)
WIDE = tuple(YW - 2 * cut for cut in YCUT)
STARTS = tuple(sum(KEEP[i] * WIDE[i] for i in range(j)) for j in range(8))
NSEND = STARTS[7]
KW = YB + 2 * WM
OFF = WM - YM

EK, EU, E1, EDGE = 0, 256, 512, 768
EKC, EUC, E1C, CEDGE = 0, 128, 256, 384

F32 = jnp.float32


def up_lane(x):
    return pltpu.roll(x, NZ - 1, axis=x.ndim - 1)


def down_lane(x):
    return pltpu.roll(x, 1, axis=x.ndim - 1)


def lanes(shape):
    return lax.broadcasted_iota(jnp.int32, shape, len(shape) - 1)


def lookup(material):
    result = jnp.zeros(material.shape, F32)
    for number in range(8):
        result = jnp.where(material == number, F32(TABLE[number]), result)
    return result


def z_faces(k, weight):
    lane = lanes(k.shape)
    upper = jnp.where(lane == NZ - 1, 0.0, up_lane(k))
    lower = jnp.where(lane == 0, 0.0, down_lane(k))
    above = weight * (k + upper)
    below = weight * (k + lower)
    return jnp.where(lane == NZ - 1, 0.0, above), above + below


def coefficients(kp, r, a, n, wx, wy, wz, below, above):
    k = kp[r, PAD + a : PAD + a + n]
    cyp = wy * (k + kp[r, PAD + a + 1 : PAD + a + n + 1])
    cym = wy * (k + kp[r, PAD + a - 1 : PAD + a + n - 1])
    cz, zsum = z_faces(k, wz)
    diag = 1.0 - (cyp + cym + zsum)
    cx = None
    if below:
        diag = diag - wx * (k + kp[r - 1, PAD + a : PAD + a + n])
    if above:
        cx = wx * (k + kp[r + 1, PAD + a : PAD + a + n])
        diag = diag - cx
    return cx, cyp, cym, cz, diag


def combine(u, r, a, n, cx_below, cx_above, cyp, cym, cz, diag):
    here = u[r, PAD + a : PAD + a + n]
    new = diag * here
    new = new + cyp * u[r, PAD + a + 1 : PAD + a + n + 1]
    new = new + cym * u[r, PAD + a - 1 : PAD + a + n - 1]
    new = new + cz * up_lane(here) + down_lane(cz * here)
    if cx_below is not None:
        new = new + cx_below * u[r - 1, PAD + a : PAD + a + n]
    if cx_above is not None:
        new = new + cx_above * u[r + 1, PAD + a : PAD + a + n]
    return new


def base(u, r, a, n, cx, cyp, cym, cz, diag, below, above):
    s = slice(a, a + n)
    return combine(
        u, r, a, n, cx[r - 1, s] if below else None, cx[r, s] if above else None, cyp[r, s], cym[r, s], cz[r, s], diag[r, s]
    )


def edge_sweep(kp, u, side, rows, a, n, wx, wy, wz):
    r = 0 if side == 0 else rows - 1
    cx, cyp, cym, cz, diag = coefficients(kp, r, a, n, wx, wy, wz, side == 1, side == 0)
    below = wx * (kp[r, PAD + a : PAD + a + n] + kp[r - 1, PAD + a : PAD + a + n]) if side == 1 else None
    return combine(u, r, a, n, below, cx, cyp, cym, cz, diag)


def each_row(count, visit):
    visit(0, False, True)

    def body(r, carry):
        visit(r, True, True)
        return carry

    lax.fori_loop(1, count - 1, body, 0)
    visit(count - 1, True, False)


def pieces(width):
    return [(a, CHUNK) for a in range(0, width, CHUNK)]


def clear_margin(ref, width):
    rows = ref.shape[0]
    ref[:, 0:PAD] = jnp.zeros((rows, PAD, NZ), F32)
    ref[:, PAD + width : PAD + width + PAD] = jnp.zeros((rows, PAD, NZ), F32)


def halve(ref, x, margin):
    total = None
    for p in range(2):
        for q in range(2):
            part = ref[2 * x + p, pl.ds(margin + q, CY, 2), :]
            total = part if total is None else total + part
    return 0.25 * total


FINE_W = (0.5 * FINE, 0.5 * FINE, 0.5 * FINE)
COARSE_W = (0.125 * COARSE, 0.125 * COARSE, 0.5 * COARSE)


def place(name):
    return lax.axis_index(name)


def block_of(h):
    return (place("y") * 2 + place("l")) * 2 + h


def lives():
    index = (place("z") * 2 + place("h")) * 2 + place("c")
    return jnp.where(index > 0, F32(1), F32(0)), jnp.where(index < 31, F32(1), F32(0))


def first_kernel(u_in, mat, src, sc, so, kp, up, edge, numbers, ends, u_sem, m_sem, s_sem):
    inside = pl.ds(PAD, NY)
    order = (0, 7, 1, 6, 2, 5, 3, 4)
    for side, r in ((0, 0), (1, ROWS - 1)):
        pltpu.make_async_copy(src.at[r], ends.at[side], s_sem.at[side]).start()
    for r in order:
        pltpu.make_async_copy(mat.at[r], numbers.at[r], m_sem.at[r]).start()
        pltpu.make_async_copy(u_in.at[0, r], up.at[r, inside], u_sem.at[r]).start()
    clear_margin(kp, NY)
    clear_margin(up, NY)
    for r in order:
        pltpu.make_async_copy(mat.at[r], numbers.at[r], m_sem.at[r]).wait()
        for a, n in pieces(NY):
            kp[r, PAD + a : PAD + a + n] = lookup(numbers[r, a : a + n])
    for r in range(ROWS):
        pltpu.make_async_copy(u_in.at[0, r], up.at[r, inside], u_sem.at[r]).wait()
    for side, r in ((0, 0), (1, ROWS - 1)):
        pltpu.make_async_copy(src.at[r], ends.at[side], s_sem.at[side]).wait()
    for side, r in ((0, 0), (1, ROWS - 1)):
        for a, n in pieces(NY):
            edge[side, EK + a : EK + a + n] = kp[r, PAD + a : PAD + a + n]
            edge[side, EU + a : EU + a + n] = up[r, PAD + a : PAD + a + n]
            edge[side, E1 + a : E1 + a + n] = edge_sweep(kp, up, side, ROWS, a, n, *FINE_W) + FINE * ends[side, a : a + n]
    c = place("c")
    sc[...] = edge[1 - c]
    so[...] = edge[c]


def coef_kernel(
    kp, up, src, cx, cyp, cym, cz, dg, ccx, ccyp, ccym, ccz, cdg, b1, cb1, ucp, csc, cso, strip, strip_h, kw, kcp, edge,
):
    clear_margin(kcp, CY)
    clear_margin(ucp, CY)
    for x in range(HALF):
        kcp[x, PAD : PAD + CY] = halve(kp, x, PAD)
        ucp[x, PAD : PAD + CY] = halve(up, x, PAD)
    clear_margin(b1, NY)
    clear_margin(cb1, CY)
    kw[:, 0:WM] = jnp.zeros((HALF, WM, NZ), F32)
    kw[:, WM + CY : WM + CY + WM] = jnp.zeros((HALF, WM, NZ), F32)
    kw[:, WM : WM + CY] = kcp[:, PAD : PAD + CY]
    h = place("h")
    strip[...] = kw[:, pl.ds(pl.multiple_of(block_of(h) * YB, 8), KW)]
    strip_h[...] = kw[:, pl.ds(pl.multiple_of(block_of(1 - h) * YB, 8), KW)]

    def make(k, u, n_all, weights, outs, target, source):
        fx, fyp, fym, fz, fd = outs

        def visit(r, below, above):
            for a, n in pieces(n_all):
                s = slice(a, a + n)
                wx = weights[0]
                above_c, yp, ym, zc, dd = coefficients(k, r, a, n, *weights, below, above)
                fyp[r, s], fym[r, s], fz[r, s], fd[r, s] = yp, ym, zc, dd
                if above:
                    fx[r, s] = above_c
                under = wx * (k[r, PAD + a : PAD + a + n] + k[r - 1, PAD + a : PAD + a + n]) if below else None
                new = combine(u, r, a, n, under, above_c, yp, ym, zc, dd)
                if source is not None:
                    new = new + FINE * source[r, s]
                target[r, PAD + a : PAD + a + n] = new

        each_row(u.shape[0], visit)

    make(kp, up, NY, FINE_W, (cx, cyp, cym, cz, dg), b1, src)
    make(kcp, ucp, CY, COARSE_W, (ccx, ccyp, ccym, ccz, cdg), cb1, None)
    c = place("c")
    for side, x in ((0, 0), (1, HALF - 1)):
        edge[side, EKC : EKC + CY] = kcp[x, PAD : PAD + CY]
        edge[side, EUC : EUC + CY] = ucp[x, PAD : PAD + CY]
        edge[side, E1C : E1C + CY] = cb1[x, PAD : PAD + CY]
    csc[...] = edge[1 - c]
    cso[...] = edge[c]


def fix_rows(target, old, swept, halo, face, rows, width):
    target[...] = swept[...]
    for side, r in ((0, 0), (1, rows - 1)):
        for a, n in pieces(width):
            s = slice(PAD + a, PAD + a + n)
            target[r, s] = swept[r, s] + face(side, a, n) * (halo(side, a, n) - old[r, s])


def halo_after(store, old, halo, later, face, live, rows, width):
    for side, r in ((0, 0), (1, rows - 1)):
        for a, n in pieces(width):
            flux = face(side, a, n) * (old[r, PAD + a : PAD + a + n] - halo(side, a, n))
            store[side, a : a + n] = live[side] * (later(side, a, n) + flux)


def full_sweep(dst, src_ref, store, face, rows, width, coefs, source):
    def visit(r, below, above):
        for a, n in pieces(width):
            new = base(src_ref, r, a, n, *coefs, below, above)
            if source is not None:
                new = new + FINE * source[r, a : a + n]
            here = src_ref[r, PAD + a : PAD + a + n]
            if not below:
                new = new + face(0, a, n) * (store[0, a : a + n] - here)
            if not above:
                new = new + face(1, a, n) * (store[1, a : a + n] - here)
            dst[r, PAD + a : PAD + a + n] = new

    each_row(rows, visit)


def reader(ref, offset=0):
    return lambda side, a, n: ref[side, offset + a : offset + a + n]


def second_kernel(
    src, sc, so, rc, ro, up, b1, strip, strip_h, cx, cyp, cym, cz, dg, u2, faces, tc, to, kown, own, got, store, edge, u1,
):
    c = place("c")
    h = place("h")
    kown[pl.ds(4 * h, HALF)] = strip[...]
    kown[pl.ds(4 * (1 - h), HALF)] = strip_h[...]
    live = lives()
    own[1 - c] = sc[...]
    own[c] = so[...]
    got[1 - c] = rc[...]
    got[c] = ro[...]
    for side in range(2):
        got[side] = got[side] * live[side]
        for a, n in pieces(NY):
            faces[side, a : a + n] = (0.5 * FINE) * (own[side, EK + a : EK + a + n] + got[side, EK + a : EK + a + n])
    clear_margin(u2, NY)
    halo_after(store, up, reader(got, EU), reader(got, E1), reader(faces), live, ROWS, NY)
    fix_rows(u1, up, b1, reader(got, EU), reader(faces), ROWS, NY)
    coefs = (cx, cyp, cym, cz, dg)
    full_sweep(u2, u1, store, reader(faces), ROWS, NY, coefs, src)
    for side, r in ((0, 0), (1, ROWS - 1)):
        for a, n in pieces(NY):
            edge[side, a : a + n] = u2[r, PAD + a : PAD + a + n]
            edge[side, NY + a : NY + a + n] = base(u2, r, a, n, *coefs, side == 1, side == 0) + FINE * src[r, a : a + n]
    tc[...] = edge[1 - c]
    to[...] = edge[c]


def middle_kernel(
    u2, src, csc, cso, crc, cro, ucp, cb1, cx, cyp, cym, cz, dg, ccx, ccyp, ccym, ccz, cdg, b3, au, own, got, cfaces, cstore, c1,
):
    c = place("c")
    live = lives()
    own[1 - c] = csc[...]
    own[c] = cso[...]
    got[1 - c] = crc[...]
    got[c] = cro[...]
    for side in range(2):
        got[side] = got[side] * live[side]
        for a, n in pieces(CY):
            cfaces[side, a : a + n] = (0.125 * COARSE) * (own[side, EKC + a : EKC + a + n] + got[side, EKC + a : EKC + a + n])
    halo_after(cstore, ucp, reader(got, EUC), reader(got, E1C), reader(cfaces), live, HALF, CY)
    fix_rows(c1, ucp, cb1, reader(got, EUC), reader(cfaces), HALF, CY)
    clear_margin(b3, NY)
    clear_margin(au, CY)

    def visit(r, below, above):
        for a, n in pieces(NY):
            b3[r, PAD + a : PAD + a + n] = base(u2, r, a, n, cx, cyp, cym, cz, dg, below, above) + FINE * src[r, a : a + n]

    each_row(ROWS, visit)
    full_sweep(au, c1, cstore, reader(cfaces), HALF, CY, (ccx, ccyp, ccym, ccz, cdg), None)


def third_kernel(
    u2, src, faces, rc, ro, b3, au, kown, keven, kodd, cx, cyp, cym, cz, dg, h_out, strips, kall, got, store, u3, f, wp,
):
    kall[0:8] = kown[...]
    kall[8:16] = keven[...]
    kall[16:24] = kodd[...]
    c = place("c")
    live = lives()
    got[1 - c] = rc[...]
    got[c] = ro[...]
    for side in range(2):
        got[side] = got[side] * live[side]
    halo_after(store, u2, reader(got), reader(got, NY), reader(faces), live, ROWS, NY)
    fix_rows(u3, u2, b3, reader(got), reader(faces), ROWS, NY)
    full_sweep(f, u3, store, reader(faces), ROWS, NY, (cx, cyp, cym, cz, dg), src)
    keep = jnp.where(place("y") + place("l") > 0, F32(1), F32(0))
    wp[:, 0:WM] = jnp.zeros((HALF, WM, NZ), F32)
    wp[:, WM + CY : WM + CY + WM] = jnp.zeros((HALF, WM, NZ), F32)
    for x in range(HALF):
        coarse = keep * au[x, PAD : PAD + CY]
        total = None
        for p in range(2):
            for q in range(2):
                part = f[2 * x + p, pl.ds(PAD + q, CY, 2), :] - coarse
                h_out[2 * x + p, pl.ds(q, CY, 2), :] = part
                total = part if total is None else total + part
        wp[x, WM : WM + CY] = 0.25 * total
    for b in range(BLOCKS):
        for x in range(HALF):
            strips[b, x * YW : (x + 1) * YW] = wp[x, b * YB + WM - YM : b * YB + WM - YM + YW]


def pack_kernel(own, even, odd):
    up = 1 - lax.rem(place("z"), 2)
    for j in range(7):
        n, cut, wide = KEEP[j], YCUT[j], WIDE[j]
        for t in range(n):
            at = STARTS[j] + t * wide
            high = own[j, (8 - n + t) * YW + cut : (8 - n + t) * YW + cut + wide]
            low = own[j, t * YW + cut : t * YW + cut + wide]
            even[at : at + wide] = jnp.where(up == 1, high, low)
            odd[at : at + wide] = jnp.where(up == 1, low, high)


def position(i):
    return 8 * (i // 4) + i % 4


def patch_kernel(kall, pkall, cxp, cyp, cym, cz, dg, kp):
    c = place("c")
    z = place("z")
    is_up = 1 - lax.rem(z, 2)
    low = jnp.where(z > 0, F32(1), F32(0))
    high = jnp.where(z < 7, F32(1), F32(0))
    first = 4 * c + 16 - XH
    kp[:, 0:PAD] = jnp.zeros((XALL, PAD, NZ), F32)
    kp[:, PAD + KW : PAD + KW + PAD] = jnp.zeros((XALL, PAD, NZ), F32)
    for core, k_ref in ((c, kall), (1 - c, pkall)):
        shift = 16 + 4 * core
        for i in range(8):
            kp[shift + position(i), PAD : PAD + KW] = k_ref[i]

            kp[shift + position(i) - 16, PAD : PAD + KW] = k_ref[8 * (1 + is_up) + i] * low
            kp[shift + position(i) + 16, PAD : PAD + KW] = k_ref[8 * (2 - is_up) + i] * high

    ycell = block_of(place("h")) * YB - WM + lax.broadcasted_iota(jnp.int32, (KW, NZ), 0)
    ymask = jnp.where((ycell >= 0) & (ycell < CY), F32(1), F32(0))
    wx, _, wz = COARSE_W

    def coef(g, carry):
        for t in range(4):
            r = 4 * g + t
            q = first + r
            k = kp[q, PAD : PAD + KW]
            a = wx * (k + kp[q, PAD + 1 : PAD + KW + 1])
            b = wx * (k + kp[q, PAD - 1 : PAD + KW - 1])
            zc, zsum = z_faces(k, wz)
            above = wx * (k + kp[q + 1, PAD : PAD + KW])
            below = wx * (k + kp[q - 1, PAD : PAD + KW])
            row = 16 * z + 4 * c - XH + r
            m = ymask * jnp.where((row >= 0) & (row < CY), F32(1), F32(0))
            m_above = ymask * jnp.where((row >= 0) & (row < CY - 1), F32(1), F32(0))
            cyp[r] = a * m
            cym[r] = b * m
            cz[r] = zc * m
            cxp[r] = above * m_above
            dg[r] = (1.0 - (a + b + zsum + above + below)) * m
        return carry

    lax.fori_loop(0, XW // 4, coef, 0)


def chain_kernel(own, part, even, odd, peven, podd, cxp, cyp, cym, cz, dg, out, w, ea, eb):
    c = place("c")
    z = place("z")
    is_up = lax.rem(z, 2) == 0
    low = jnp.where(z > 0, F32(1), F32(0))
    high = jnp.where(z < 7, F32(1), F32(0))
    first = 4 * c + 16 - XH

    for core, mine, e_ref, o_ref in ((c, own, even, odd), (1 - c, part, peven, podd)):
        shift = 16 + 4 * core
        for j in range(7):
            for i in range(8):
                w[j, shift + position(i), OFF : OFF + YW] = mine[j, i * YW : (i + 1) * YW]

        def fill(from_below, from_above):
            for j in range(7):
                n, cut, wide = KEEP[j], YCUT[j], WIDE[j]
                for t in range(n):
                    at = STARTS[j] + t * wide
                    w[j, shift + position(8 - n + t) - 16, OFF + cut : OFF + cut + wide] = from_below[at : at + wide] * low
                    w[j, shift + position(t) + 16, OFF + cut : OFF + cut + wide] = from_above[at : at + wide] * high

        @pl.when(is_up)
        def _():
            fill(o_ref, e_ref)

        @pl.when(jnp.logical_not(is_up))
        def _():
            fill(e_ref, o_ref)

    for r in range(XW):
        ea[r, PAD : PAD + KW] = w[0, first + r]

    def halved(lo, hi, visit):
        half = (hi - lo) // 2

        def body(g, carry):
            for t in range(half):
                visit(lo + g * half + t)
            return carry

        lax.fori_loop(0, 2, body, 0)

    def sweep(src, dst, number):
        cut = 0 if number <= 5 else 8
        s = slice(cut, KW - cut)
        n = KW - 2 * cut

        def visit(r):
            here = src[r, PAD + cut : PAD + cut + n]
            zc = cz[r, s]
            new = dg[r, s] * here + cyp[r, s] * src[r, PAD + cut + 1 : PAD + cut + n + 1]
            new = new + cym[r, s] * src[r, PAD + cut - 1 : PAD + cut + n - 1]
            new = new + (cxp[r - 1, s] * src[r - 1, PAD + cut : PAD + cut + n] + cxp[r, s] * src[r + 1, PAD + cut : PAD + cut + n])
            dst[r, PAD + cut : PAD + cut + n] = new + (zc * up_lane(here) + down_lane(zc * here))

        halved(number, XW - number, visit)

    out[2:4] = jnp.zeros((2, HALF, YB, NZ), F32)
    for k in range(1, 8):
        sweep(ea, eb, 2 * k - 1)
        sweep(eb, ea, 2 * k)
        m = (k + 1) % SLABS
        for side in range(2):
            for i in range(HALF):
                out[2 * m + side, i] = ea[XH + 8 * side + i, PAD + WM : PAD + WM + YB]
        if k < 7:
            cut = 8 if k >= 3 else 0
            s = slice(PAD + cut, PAD + KW - cut)

            def add(r):
                ea[r, s] = ea[r, s] + w[k, first + r, cut : KW - cut]

            halved(2 * k, XW - 2 * k, add)


def last_kernel(h_in, y_in, out):
    for x in range(HALF):
        fix = y_in[:, x].reshape(CY, NZ)
        for p in range(2):
            for q in range(2):
                out[0, 2 * x + p, pl.ds(q, CY, 2), :] = h_in[2 * x + p, pl.ds(q, CY, 2), :] + fix


def call(kernel, outs, scratch, *operands, limit=6, specs=None):
    vmem = pl.BlockSpec(memory_space=pltpu.VMEM)
    return pl.pallas_call(
        kernel,
        out_shape=[jax.ShapeDtypeStruct(s, F32) for s in outs],
        in_specs=specs or [vmem] * len(operands),
        out_specs=[vmem] * len(outs),
        scratch_shapes=[s if callable(getattr(s, "get_ref_aval", None)) else pltpu.VMEM(s, F32) for s in scratch],
        compiler_params=pltpu.CompilerParams(vmem_limit_bytes=limit * 1024 * 1024),
    )(*operands)


def pairs(n, odd):
    found = []
    for i in range(odd, n - 1, 2):
        found += [(i, i + 1), (i + 1, i)]
    if odd:
        found += [(0, n - 1), (n - 1, 0)]
    return found


SPACE = ("z", "h", "c")
PLANE = ("y", "l", "h")


def steps(starts, material, source):
    fine = (ROWS, NY, NZ)
    crs = (HALF, CY, NZ)
    padded = (ROWS, NY + 2 * PAD, NZ)
    cpad = (HALF, CY + 2 * PAD, NZ)
    strip_shape = (HALF, KW, NZ)

    def swap_c(x):
        return lax.ppermute(x, "c", pairs(2, 0))

    def swap_o(x):
        return lax.ppermute(x, SPACE, pairs(32, 1))

    dma = pltpu.SemaphoreType.DMA
    sc, so, kp, up = call(
        first_kernel,
        ((EDGE, NZ), (EDGE, NZ), padded, padded),
        ((2, EDGE, NZ), pltpu.VMEM(fine, jnp.int32), (2, NY, NZ), dma((ROWS,)), dma((ROWS,)), dma((2,))),
        *(pltpu.with_memory_space_constraint(x, pltpu.HBM) for x in (starts, material, source)),
        specs=[pl.BlockSpec(memory_space=pltpu.HBM)] * 3,
    )
    rc = swap_c(sc)
    ro = swap_o(so)
    edges = (CEDGE, NZ)
    *coefs, b1, cb1, ucp, csc, cso, strip, strip_h = call(
        coef_kernel, (fine,) * 5 + (crs,) * 5 + (padded, cpad, cpad, edges, edges, strip_shape, strip_shape),
        ((HALF, CY + 2 * WM, NZ), cpad, (2, CEDGE, NZ)),
        kp, up, source,
    )
    strip_h = lax.ppermute(strip_h, "h", pairs(2, 0))
    strip_h, csc, cso = lax.optimization_barrier((strip_h, csc, cso))
    cro = swap_o(cso)
    crc = swap_c(csc)
    u2, faces, tc, to, kown = call(
        second_kernel,
        (padded, (2, NY, NZ), (2 * NY, NZ), (2 * NY, NZ), (8, KW, NZ)),
        ((2, EDGE, NZ), (2, EDGE, NZ), (2, NY, NZ), (2, 2 * NY, NZ), padded),
        source, sc, so, rc, ro, up, b1, strip, strip_h, *coefs[:5],
    )
    rc2 = swap_c(tc)
    ro2 = swap_o(to)
    keven = lax.ppermute(kown, "z", pairs(8, 0))
    kodd = lax.ppermute(kown, "z", pairs(8, 1))
    b3, au = call(
        middle_kernel, (padded, cpad), ((2, CEDGE, NZ), (2, CEDGE, NZ), (2, CY, NZ), (2, CY, NZ), cpad),
        u2, source, csc, cso, crc, cro, ucp, cb1, *coefs,
    )
    moved, strips, kall = call(
        third_kernel,
        (fine, (BLOCKS, HALF * YW, NZ), (24, KW, NZ)),
        ((2, 2 * NY, NZ), (2, NY, NZ), padded, padded, (HALF, CY + 2 * WM, NZ)),
        u2, source, faces, rc2, ro2, b3, au, kown, keven, kodd, *coefs[:5],
    )
    own = lax.all_to_all(strips, PLANE, 0, 0, tiled=True)
    own, moved, kall = lax.optimization_barrier((own, moved, kall))
    own = own.reshape(SLABS, 8 * YW, NZ)
    even, odd = call(pack_kernel, ((NSEND, NZ), (NSEND, NZ)), (), own)
    even = lax.ppermute(even, "z", pairs(8, 0))
    odd = lax.ppermute(odd, "z", pairs(8, 1))
    part = swap_c(own)
    pkall = swap_c(kall)
    moved = lax.ppermute(moved, ("y", "l"), [(i, (i + 1) % 8) for i in range(8)])
    peven = swap_c(even)
    podd = swap_c(odd)
    dom = (XW + 1, KW + 2 * PAD, NZ)
    flat = (XW, KW, NZ)
    patch = call(patch_kernel, (flat,) * 5, ((XALL, KW + 2 * PAD, NZ),), kall, pkall)
    (fixes,) = call(
        chain_kernel, ((BLOCKS, HALF, YB, NZ),), ((7, XALL, KW, NZ), dom, dom),
        own, part, even, odd, peven, podd, *patch, limit=12,
    )
    fixes = lax.all_to_all(fixes, PLANE, 0, 0, tiled=True)
    (result,) = call(last_kernel, ((1, ROWS, NY, NZ),), (), moved, fixes)
    return result


def solution(mesh):
    refined = Mesh(mesh.devices.reshape(SIZES), AXES)
    in_specs = (P(("y", "l"), SPACE, None, None), P(SPACE, None, None), P(SPACE, None, None))
    out_specs = P(("y", "l"), SPACE, None, None)
    return jax.shard_map(steps, mesh=refined, in_specs=in_specs, out_specs=out_specs, check_vma=False)
```

```python
import jax
import jax.numpy as jnp
from jax import lax
from jax.experimental import pallas as pl
from jax.experimental.pallas import tpu as pltpu
from jax.sharding import Mesh, PartitionSpec as P


SIZES = (4, 2, 8, 2, 2)
AXES = ("y", "l", "z", "h", "c")
SLABS = 8
ROWS = 8
NY = 256
NZ = 128
HALF = ROWS // 2
CY = NY // 2
PAD = 8
CHUNK = 64
FINE = 0.15
COARSE = 0.3
TABLE = (1.0, 0.72, 0.52, 0.37, 0.26, 0.18, 0.13, 0.09)

BLOCKS = 16
YB = CY // BLOCKS
YM = 14
WM = 16
YW = YB + 2 * YM
XH = 14
XW = 12 + 2 * XH
XALL = 48
KEEP = (8, 8, 6, 4, 4, 4, 2)
YCUT = (0, 2, 4, 6, 8, 10, 12)
WIDE = tuple(YW - 2 * cut for cut in YCUT)
STARTS = tuple(sum(KEEP[i] * WIDE[i] for i in range(j)) for j in range(8))
NSEND = STARTS[7]
KW = YB + 2 * WM
OFF = WM - YM

EK, EU, E1, EDGE = 0, 256, 512, 768
EKC, EUC, E1C, CEDGE = 0, 128, 256, 384

F32 = jnp.float32


def up_lane(x):
    return pltpu.roll(x, NZ - 1, axis=x.ndim - 1)


def down_lane(x):
    return pltpu.roll(x, 1, axis=x.ndim - 1)


def lanes(shape):
    return lax.broadcasted_iota(jnp.int32, shape, len(shape) - 1)


def lookup(material):
    result = jnp.zeros(material.shape, F32)
    for number in range(8):
        result = jnp.where(material == number, F32(TABLE[number]), result)
    return result


def z_faces(k, weight):
    lane = lanes(k.shape)
    upper = jnp.where(lane == NZ - 1, 0.0, up_lane(k))
    lower = jnp.where(lane == 0, 0.0, down_lane(k))
    above = weight * (k + upper)
    below = weight * (k + lower)
    return jnp.where(lane == NZ - 1, 0.0, above), above + below


def coefficients(kp, r, a, n, wx, wy, wz, below, above):
    k = kp[r, PAD + a : PAD + a + n]
    cyp = wy * (k + kp[r, PAD + a + 1 : PAD + a + n + 1])
    cym = wy * (k + kp[r, PAD + a - 1 : PAD + a + n - 1])
    cz, zsum = z_faces(k, wz)
    diag = 1.0 - (cyp + cym + zsum)
    cx = None
    if below:
        diag = diag - wx * (k + kp[r - 1, PAD + a : PAD + a + n])
    if above:
        cx = wx * (k + kp[r + 1, PAD + a : PAD + a + n])
        diag = diag - cx
    return cx, cyp, cym, cz, diag


def combine(u, r, a, n, cx_below, cx_above, cyp, cym, cz, diag):
    here = u[r, PAD + a : PAD + a + n]
    new = diag * here
    new = new + cyp * u[r, PAD + a + 1 : PAD + a + n + 1]
    new = new + cym * u[r, PAD + a - 1 : PAD + a + n - 1]
    new = new + cz * up_lane(here) + down_lane(cz * here)
    if cx_below is not None:
        new = new + cx_below * u[r - 1, PAD + a : PAD + a + n]
    if cx_above is not None:
        new = new + cx_above * u[r + 1, PAD + a : PAD + a + n]
    return new


def base(u, r, a, n, cx, cyp, cym, cz, diag, below, above):
    s = slice(a, a + n)
    return combine(
        u, r, a, n, cx[r - 1, s] if below else None, cx[r, s] if above else None, cyp[r, s], cym[r, s], cz[r, s], diag[r, s]
    )


def edge_sweep(kp, u, side, rows, a, n, wx, wy, wz):
    r = 0 if side == 0 else rows - 1
    cx, cyp, cym, cz, diag = coefficients(kp, r, a, n, wx, wy, wz, side == 1, side == 0)
    below = wx * (kp[r, PAD + a : PAD + a + n] + kp[r - 1, PAD + a : PAD + a + n]) if side == 1 else None
    return combine(u, r, a, n, below, cx, cyp, cym, cz, diag)


def each_row(count, visit):
    visit(0, False, True)

    def body(r, carry):
        visit(r, True, True)
        return carry

    lax.fori_loop(1, count - 1, body, 0)
    visit(count - 1, True, False)


def pieces(width):
    return [(a, CHUNK) for a in range(0, width, CHUNK)]


def clear_margin(ref, width):
    rows = ref.shape[0]
    ref[:, 0:PAD] = jnp.zeros((rows, PAD, NZ), F32)
    ref[:, PAD + width : PAD + width + PAD] = jnp.zeros((rows, PAD, NZ), F32)


def halve(ref, x, margin):
    total = None
    for p in range(2):
        for q in range(2):
            part = ref[2 * x + p, pl.ds(margin + q, CY, 2), :]
            total = part if total is None else total + part
    return 0.25 * total


FINE_W = (0.5 * FINE, 0.5 * FINE, 0.5 * FINE)
COARSE_W = (0.125 * COARSE, 0.125 * COARSE, 0.5 * COARSE)


def place(name):
    return lax.axis_index(name)


def block_of(h):
    return (place("y") * 2 + place("l")) * 2 + h


def lives():
    index = (place("z") * 2 + place("h")) * 2 + place("c")
    return jnp.where(index > 0, F32(1), F32(0)), jnp.where(index < 31, F32(1), F32(0))


def first_kernel(u_in, mat, src, sc, so, kp, up, edge, numbers, ends, u_sem, m_sem, s_sem):
    inside = pl.ds(PAD, NY)
    order = (0, 7, 1, 6, 2, 5, 3, 4)
    for side, r in ((0, 0), (1, ROWS - 1)):
        pltpu.make_async_copy(src.at[r], ends.at[side], s_sem.at[side]).start()
    for r in order:
        pltpu.make_async_copy(mat.at[r], numbers.at[r], m_sem.at[r]).start()
        pltpu.make_async_copy(u_in.at[0, r], up.at[r, inside], u_sem.at[r]).start()
    clear_margin(kp, NY)
    clear_margin(up, NY)
    for r in order:
        pltpu.make_async_copy(mat.at[r], numbers.at[r], m_sem.at[r]).wait()
        for a, n in pieces(NY):
            kp[r, PAD + a : PAD + a + n] = lookup(numbers[r, a : a + n])
    for r in range(ROWS):
        pltpu.make_async_copy(u_in.at[0, r], up.at[r, inside], u_sem.at[r]).wait()
    for side, r in ((0, 0), (1, ROWS - 1)):
        pltpu.make_async_copy(src.at[r], ends.at[side], s_sem.at[side]).wait()
    for side, r in ((0, 0), (1, ROWS - 1)):
        for a, n in pieces(NY):
            edge[side, EK + a : EK + a + n] = kp[r, PAD + a : PAD + a + n]
            edge[side, EU + a : EU + a + n] = up[r, PAD + a : PAD + a + n]
            edge[side, E1 + a : E1 + a + n] = edge_sweep(kp, up, side, ROWS, a, n, *FINE_W) + FINE * ends[side, a : a + n]
    c = place("c")
    sc[...] = edge[1 - c]
    so[...] = edge[c]


def coef_kernel(
    kp, up, src, cx, cyp, cym, cz, dg, ccx, ccyp, ccym, ccz, cdg, b1, b2, cb1, ucp, csc, cso, strip, strip_h, kw, kcp, edge,
):
    clear_margin(kcp, CY)
    clear_margin(ucp, CY)
    for x in range(HALF):
        kcp[x, PAD : PAD + CY] = halve(kp, x, PAD)
        ucp[x, PAD : PAD + CY] = halve(up, x, PAD)
    clear_margin(b1, NY)
    clear_margin(b2, NY)
    clear_margin(cb1, CY)
    kw[:, 0:WM] = jnp.zeros((HALF, WM, NZ), F32)
    kw[:, WM + CY : WM + CY + WM] = jnp.zeros((HALF, WM, NZ), F32)
    kw[:, WM : WM + CY] = kcp[:, PAD : PAD + CY]
    h = place("h")
    strip[...] = kw[:, pl.ds(pl.multiple_of(block_of(h) * YB, 8), KW)]
    strip_h[...] = kw[:, pl.ds(pl.multiple_of(block_of(1 - h) * YB, 8), KW)]

    def make(k, u, n_all, weights, outs, target, source):
        fx, fyp, fym, fz, fd = outs

        def visit(r, below, above):
            for a, n in pieces(n_all):
                s = slice(a, a + n)
                wx = weights[0]
                above_c, yp, ym, zc, dd = coefficients(k, r, a, n, *weights, below, above)
                fyp[r, s], fym[r, s], fz[r, s], fd[r, s] = yp, ym, zc, dd
                if above:
                    fx[r, s] = above_c
                under = wx * (k[r, PAD + a : PAD + a + n] + k[r - 1, PAD + a : PAD + a + n]) if below else None
                new = combine(u, r, a, n, under, above_c, yp, ym, zc, dd)
                if source is not None:
                    new = new + FINE * source[r, s]
                target[r, PAD + a : PAD + a + n] = new

        each_row(u.shape[0], visit)

    make(kp, up, NY, FINE_W, (cx, cyp, cym, cz, dg), b1, src)
    inner_rows(b2, b1, (cx, cyp, cym, cz, dg), src)
    make(kcp, ucp, CY, COARSE_W, (ccx, ccyp, ccym, ccz, cdg), cb1, None)
    c = place("c")
    for side, x in ((0, 0), (1, HALF - 1)):
        edge[side, EKC : EKC + CY] = kcp[x, PAD : PAD + CY]
        edge[side, EUC : EUC + CY] = ucp[x, PAD : PAD + CY]
        edge[side, E1C : E1C + CY] = cb1[x, PAD : PAD + CY]
    csc[...] = edge[1 - c]
    cso[...] = edge[c]


def inner_rows(dst, src_ref, coefs, source):
    def body(r, carry):
        for a, n in pieces(NY):
            dst[r, PAD + a : PAD + a + n] = base(src_ref, r, a, n, *coefs, True, True) + FINE * source[r, a : a + n]
        return carry

    lax.fori_loop(2, ROWS - 2, body, 0)


def outer_rows(dst, src_ref, store, face, coefs, source):
    for r in (1, ROWS - 2, 0, ROWS - 1):
        below, above = r > 0, r < ROWS - 1
        for a, n in pieces(NY):
            new = base(src_ref, r, a, n, *coefs, below, above) + FINE * source[r, a : a + n]
            here = src_ref[r, PAD + a : PAD + a + n]
            if not below:
                new = new + face(0, a, n) * (store[0, a : a + n] - here)
            if not above:
                new = new + face(1, a, n) * (store[1, a : a + n] - here)
            dst[r, PAD + a : PAD + a + n] = new


def fix_rows(target, old, halo, face, rows, width):
    for side, r in ((0, 0), (1, rows - 1)):
        for a, n in pieces(width):
            s = slice(PAD + a, PAD + a + n)
            target[r, s] = target[r, s] + face(side, a, n) * (halo(side, a, n) - old[r, s])


def halo_after(store, old, halo, later, face, live, rows, width):
    for side, r in ((0, 0), (1, rows - 1)):
        for a, n in pieces(width):
            flux = face(side, a, n) * (old[r, PAD + a : PAD + a + n] - halo(side, a, n))
            store[side, a : a + n] = live[side] * (later(side, a, n) + flux)


def full_sweep(dst, src_ref, store, face, rows, width, coefs, source):
    def visit(r, below, above):
        for a, n in pieces(width):
            new = base(src_ref, r, a, n, *coefs, below, above)
            if source is not None:
                new = new + FINE * source[r, a : a + n]
            here = src_ref[r, PAD + a : PAD + a + n]
            if not below:
                new = new + face(0, a, n) * (store[0, a : a + n] - here)
            if not above:
                new = new + face(1, a, n) * (store[1, a : a + n] - here)
            dst[r, PAD + a : PAD + a + n] = new

    each_row(rows, visit)


def reader(ref, offset=0):
    return lambda side, a, n: ref[side, offset + a : offset + a + n]


def second_kernel(
    src, sc, so, rc, ro, up, b1, b2, strip, strip_h, cx, cyp, cym, cz, dg, u1, u2, faces, tc, to, kown, own, got, store, edge,
):
    c = place("c")
    h = place("h")
    kown[pl.ds(4 * h, HALF)] = strip[...]
    kown[pl.ds(4 * (1 - h), HALF)] = strip_h[...]
    live = lives()
    own[1 - c] = sc[...]
    own[c] = so[...]
    got[1 - c] = rc[...]
    got[c] = ro[...]
    for side in range(2):
        got[side] = got[side] * live[side]
        for a, n in pieces(NY):
            faces[side, a : a + n] = (0.5 * FINE) * (own[side, EK + a : EK + a + n] + got[side, EK + a : EK + a + n])
    halo_after(store, up, reader(got, EU), reader(got, E1), reader(faces), live, ROWS, NY)
    fix_rows(u1, up, reader(got, EU), reader(faces), ROWS, NY)
    coefs = (cx, cyp, cym, cz, dg)
    outer_rows(u2, u1, store, reader(faces), coefs, src)
    for side, r in ((0, 0), (1, ROWS - 1)):
        for a, n in pieces(NY):
            edge[side, a : a + n] = u2[r, PAD + a : PAD + a + n]
            edge[side, NY + a : NY + a + n] = base(u2, r, a, n, *coefs, side == 1, side == 0) + FINE * src[r, a : a + n]
    tc[...] = edge[1 - c]
    to[...] = edge[c]


def middle_kernel(
    u2, src, csc, cso, crc, cro, ucp, cb1, cx, cyp, cym, cz, dg, ccx, ccyp, ccym, ccz, cdg, b3, b4, au, own, got, cfaces, cstore, c1,
):
    c = place("c")
    live = lives()
    own[1 - c] = csc[...]
    own[c] = cso[...]
    got[1 - c] = crc[...]
    got[c] = cro[...]
    for side in range(2):
        got[side] = got[side] * live[side]
        for a, n in pieces(CY):
            cfaces[side, a : a + n] = (0.125 * COARSE) * (own[side, EKC + a : EKC + a + n] + got[side, EKC + a : EKC + a + n])
    halo_after(cstore, ucp, reader(got, EUC), reader(got, E1C), reader(cfaces), live, HALF, CY)
    c1[...] = cb1[...]
    fix_rows(c1, ucp, reader(got, EUC), reader(cfaces), HALF, CY)
    clear_margin(b3, NY)
    clear_margin(b4, NY)
    clear_margin(au, CY)

    def visit(r, below, above):
        for a, n in pieces(NY):
            b3[r, PAD + a : PAD + a + n] = base(u2, r, a, n, cx, cyp, cym, cz, dg, below, above) + FINE * src[r, a : a + n]

    each_row(ROWS, visit)
    inner_rows(b4, b3, (cx, cyp, cym, cz, dg), src)
    full_sweep(au, c1, cstore, reader(cfaces), HALF, CY, (ccx, ccyp, ccym, ccz, cdg), None)


def third_kernel(
    u2, src, faces, rc, ro, b3, b4, au, cx, cyp, cym, cz, dg, u3, f, h_out, strips, got, store, wp,
):
    c = place("c")
    live = lives()
    got[1 - c] = rc[...]
    got[c] = ro[...]
    for side in range(2):
        got[side] = got[side] * live[side]
    halo_after(store, u2, reader(got), reader(got, NY), reader(faces), live, ROWS, NY)
    fix_rows(u3, u2, reader(got), reader(faces), ROWS, NY)
    outer_rows(f, u3, store, reader(faces), (cx, cyp, cym, cz, dg), src)
    keep = jnp.where(place("y") + place("l") > 0, F32(1), F32(0))
    wp[:, 0:WM] = jnp.zeros((HALF, WM, NZ), F32)
    wp[:, WM + CY : WM + CY + WM] = jnp.zeros((HALF, WM, NZ), F32)
    for x in range(HALF):
        coarse = keep * au[x, PAD : PAD + CY]
        total = None
        for p in range(2):
            for q in range(2):
                part = f[2 * x + p, pl.ds(PAD + q, CY, 2), :] - coarse
                h_out[2 * x + p, pl.ds(q, CY, 2), :] = part
                total = part if total is None else total + part
        wp[x, WM : WM + CY] = 0.25 * total
    for b in range(BLOCKS):
        for x in range(HALF):
            strips[b, x * YW : (x + 1) * YW] = wp[x, b * YB + WM - YM : b * YB + WM - YM + YW]


def pack_kernel(own, kown, keven, kodd, even, odd, kall):
    kall[0:8] = kown[...]
    kall[8:16] = keven[...]
    kall[16:24] = kodd[...]
    up = 1 - lax.rem(place("z"), 2)
    for j in range(7):
        n, cut, wide = KEEP[j], YCUT[j], WIDE[j]
        for t in range(n):
            at = STARTS[j] + t * wide
            high = own[j, (8 - n + t) * YW + cut : (8 - n + t) * YW + cut + wide]
            low = own[j, t * YW + cut : t * YW + cut + wide]
            even[at : at + wide] = jnp.where(up == 1, high, low)
            odd[at : at + wide] = jnp.where(up == 1, low, high)


def position(i):
    return 8 * (i // 4) + i % 4


def patch_kernel(kall, pkall, cxp, cyp, cym, cz, dg, kp):
    c = place("c")
    z = place("z")
    is_up = 1 - lax.rem(z, 2)
    low = jnp.where(z > 0, F32(1), F32(0))
    high = jnp.where(z < 7, F32(1), F32(0))
    first = 4 * c + 16 - XH
    kp[:, 0:PAD] = jnp.zeros((XALL, PAD, NZ), F32)
    kp[:, PAD + KW : PAD + KW + PAD] = jnp.zeros((XALL, PAD, NZ), F32)
    for core, k_ref in ((c, kall), (1 - c, pkall)):
        shift = 16 + 4 * core
        for i in range(8):
            kp[shift + position(i), PAD : PAD + KW] = k_ref[i]

            kp[shift + position(i) - 16, PAD : PAD + KW] = k_ref[8 * (1 + is_up) + i] * low
            kp[shift + position(i) + 16, PAD : PAD + KW] = k_ref[8 * (2 - is_up) + i] * high

    ycell = block_of(place("h")) * YB - WM + lax.broadcasted_iota(jnp.int32, (KW, NZ), 0)
    ymask = jnp.where((ycell >= 0) & (ycell < CY), F32(1), F32(0))
    wx, _, wz = COARSE_W

    def coef(g, carry):
        for t in range(4):
            r = 4 * g + t
            q = first + r
            k = kp[q, PAD : PAD + KW]
            a = wx * (k + kp[q, PAD + 1 : PAD + KW + 1])
            b = wx * (k + kp[q, PAD - 1 : PAD + KW - 1])
            zc, zsum = z_faces(k, wz)
            above = wx * (k + kp[q + 1, PAD : PAD + KW])
            below = wx * (k + kp[q - 1, PAD : PAD + KW])
            row = 16 * z + 4 * c - XH + r
            m = ymask * jnp.where((row >= 0) & (row < CY), F32(1), F32(0))
            m_above = ymask * jnp.where((row >= 0) & (row < CY - 1), F32(1), F32(0))
            cyp[r] = a * m
            cym[r] = b * m
            cz[r] = zc * m
            cxp[r] = above * m_above
            dg[r] = (1.0 - (a + b + zsum + above + below)) * m
        return carry

    lax.fori_loop(0, XW // 4, coef, 0)


def chain_kernel(own, part, even, odd, peven, podd, cxp, cyp, cym, cz, dg, out, w, ea, eb):
    c = place("c")
    z = place("z")
    is_up = lax.rem(z, 2) == 0
    low = jnp.where(z > 0, F32(1), F32(0))
    high = jnp.where(z < 7, F32(1), F32(0))
    first = 4 * c + 16 - XH

    for core, mine, e_ref, o_ref in ((c, own, even, odd), (1 - c, part, peven, podd)):
        shift = 16 + 4 * core
        for j in range(7):
            for i in range(8):
                w[j, shift + position(i), OFF : OFF + YW] = mine[j, i * YW : (i + 1) * YW]

        def fill(from_below, from_above):
            for j in range(7):
                n, cut, wide = KEEP[j], YCUT[j], WIDE[j]
                for t in range(n):
                    at = STARTS[j] + t * wide
                    w[j, shift + position(8 - n + t) - 16, OFF + cut : OFF + cut + wide] = from_below[at : at + wide] * low
                    w[j, shift + position(t) + 16, OFF + cut : OFF + cut + wide] = from_above[at : at + wide] * high

        @pl.when(is_up)
        def _():
            fill(o_ref, e_ref)

        @pl.when(jnp.logical_not(is_up))
        def _():
            fill(e_ref, o_ref)

    for r in range(XW):
        ea[r, PAD : PAD + KW] = w[0, first + r]

    def each(lo, hi, visit):
        for r in range(lo, hi):
            visit(r)

    def sweep(src, dst, number):
        cut = 0 if number <= 5 else 8
        s = slice(cut, KW - cut)
        n = KW - 2 * cut

        def visit(r):
            here = src[r, PAD + cut : PAD + cut + n]
            zc = cz[r, s]
            new = dg[r, s] * here + cyp[r, s] * src[r, PAD + cut + 1 : PAD + cut + n + 1]
            new = new + cym[r, s] * src[r, PAD + cut - 1 : PAD + cut + n - 1]
            new = new + (cxp[r - 1, s] * src[r - 1, PAD + cut : PAD + cut + n] + cxp[r, s] * src[r + 1, PAD + cut : PAD + cut + n])
            dst[r, PAD + cut : PAD + cut + n] = new + (zc * up_lane(here) + down_lane(zc * here))

        each(number, XW - number, visit)

    out[2:4] = jnp.zeros((2, HALF, YB, NZ), F32)
    for k in range(1, 8):
        sweep(ea, eb, 2 * k - 1)
        sweep(eb, ea, 2 * k)
        m = (k + 1) % SLABS
        for side in range(2):
            for i in range(HALF):
                out[2 * m + side, i] = ea[XH + 8 * side + i, PAD + WM : PAD + WM + YB]
        if k < 7:
            cut = 8 if k >= 3 else 0
            s = slice(PAD + cut, PAD + KW - cut)

            def add(r):
                ea[r, s] = ea[r, s] + w[k, first + r, cut : KW - cut]

            each(2 * k, XW - 2 * k, add)


def last_kernel(h_in, y_in, out):
    for x in range(HALF):
        fix = y_in[:, x].reshape(CY, NZ)
        for p in range(2):
            for q in range(2):
                out[0, 2 * x + p, pl.ds(q, CY, 2), :] = h_in[2 * x + p, pl.ds(q, CY, 2), :] + fix


def call(kernel, outs, scratch, *operands, limit=6, specs=None, alias=()):
    vmem = pl.BlockSpec(memory_space=pltpu.VMEM)
    return pl.pallas_call(
        kernel,
        out_shape=[jax.ShapeDtypeStruct(s, F32) for s in outs],
        in_specs=specs or [vmem] * len(operands),
        out_specs=[vmem] * len(outs),
        scratch_shapes=[s if callable(getattr(s, "get_ref_aval", None)) else pltpu.VMEM(s, F32) for s in scratch],
        input_output_aliases=dict(alias),
        compiler_params=pltpu.CompilerParams(vmem_limit_bytes=limit * 1024 * 1024),
    )(*operands)


def pairs(n, odd):
    found = []
    for i in range(odd, n - 1, 2):
        found += [(i, i + 1), (i + 1, i)]
    if odd:
        found += [(0, n - 1), (n - 1, 0)]
    return found


SPACE = ("z", "h", "c")
PLANE = ("y", "l", "h")


def steps(starts, material, source):
    fine = (ROWS, NY, NZ)
    crs = (HALF, CY, NZ)
    padded = (ROWS, NY + 2 * PAD, NZ)
    cpad = (HALF, CY + 2 * PAD, NZ)
    strip_shape = (HALF, KW, NZ)

    def swap_c(x):
        return lax.ppermute(x, "c", pairs(2, 0))

    def swap_o(x):
        return lax.ppermute(x, SPACE, pairs(32, 1))

    dma = pltpu.SemaphoreType.DMA
    sc, so, kp, up = call(
        first_kernel,
        ((EDGE, NZ), (EDGE, NZ), padded, padded),
        ((2, EDGE, NZ), pltpu.VMEM(fine, jnp.int32), (2, NY, NZ), dma((ROWS,)), dma((ROWS,)), dma((2,))),
        *(pltpu.with_memory_space_constraint(x, pltpu.HBM) for x in (starts, material, source)),
        specs=[pl.BlockSpec(memory_space=pltpu.HBM)] * 3,
    )
    ro = swap_o(so)
    rc = swap_c(sc)
    edges = (CEDGE, NZ)
    *coefs, b1, b2, cb1, ucp, csc, cso, strip, strip_h = call(
        coef_kernel, (fine,) * 5 + (crs,) * 5 + (padded, padded, cpad, cpad, edges, edges, strip_shape, strip_shape),
        ((HALF, CY + 2 * WM, NZ), cpad, (2, CEDGE, NZ)),
        kp, up, source,
    )
    strip_h = lax.ppermute(strip_h, "h", pairs(2, 0))
    crc = swap_c(csc)
    strip_h, cso = lax.optimization_barrier((strip_h, cso))
    cro = swap_o(cso)
    _, u2, faces, tc, to, kown = call(
        second_kernel,
        (padded, padded, (2, NY, NZ), (2 * NY, NZ), (2 * NY, NZ), (8, KW, NZ)),
        ((2, EDGE, NZ), (2, EDGE, NZ), (2, NY, NZ), (2, 2 * NY, NZ)),
        source, sc, so, rc, ro, up, b1, b2, strip, strip_h, *coefs[:5], alias=((6, 0), (7, 1)),
    )
    ro2 = swap_o(to)
    rc2 = swap_c(tc)
    keven = lax.ppermute(kown, "z", pairs(8, 0))
    kodd = lax.ppermute(kown, "z", pairs(8, 1))
    b3, b4, au = call(
        middle_kernel, (padded, padded, cpad), ((2, CEDGE, NZ), (2, CEDGE, NZ), (2, CY, NZ), (2, CY, NZ), cpad),
        u2, source, csc, cso, crc, cro, ucp, cb1, *coefs,
    )
    _, _, moved, strips = call(
        third_kernel,
        (padded, padded, fine, (BLOCKS, HALF * YW, NZ)),
        ((2, 2 * NY, NZ), (2, NY, NZ), (HALF, CY + 2 * WM, NZ)),
        u2, source, faces, rc2, ro2, b3, b4, au, *coefs[:5], alias=((5, 0), (6, 1)),
    )
    own = lax.all_to_all(strips, PLANE, 0, 0, tiled=True)
    own, moved = lax.optimization_barrier((own, moved))
    own = own.reshape(SLABS, 8 * YW, NZ)
    even, odd, kall = call(pack_kernel, ((NSEND, NZ), (NSEND, NZ), (24, KW, NZ)), (), own, kown, keven, kodd)
    even = lax.ppermute(even, "z", pairs(8, 0))
    odd = lax.ppermute(odd, "z", pairs(8, 1))
    part = swap_c(own)
    pkall = swap_c(kall)
    moved = lax.ppermute(moved, ("y", "l"), [(i, (i + 1) % 8) for i in range(8)])
    peven = swap_c(even)
    podd = swap_c(odd)
    dom = (XW + 1, KW + 2 * PAD, NZ)
    flat = (XW, KW, NZ)
    patch = call(patch_kernel, (flat,) * 5, ((XALL, KW + 2 * PAD, NZ),), kall, pkall)
    (fixes,) = call(
        chain_kernel, ((BLOCKS, HALF, YB, NZ),), ((7, XALL, KW, NZ), dom, dom),
        own, part, even, odd, peven, podd, *patch, limit=12,
    )
    fixes = lax.all_to_all(fixes, PLANE, 0, 0, tiled=True)
    (result,) = call(last_kernel, ((1, ROWS, NY, NZ),), (), moved, fixes)
    return result


def solution(mesh):
    refined = Mesh(mesh.devices.reshape(SIZES), AXES)
    in_specs = (P(("y", "l"), SPACE, None, None), P(SPACE, None, None), P(SPACE, None, None))
    out_specs = P(("y", "l"), SPACE, None, None)
    return jax.shard_map(steps, mesh=refined, in_specs=in_specs, out_specs=out_specs, check_vma=False)
```

```python
import jax
import jax.numpy as jnp
from jax import lax
from jax.experimental import pallas as pl
from jax.experimental.pallas import tpu as pltpu
from jax.sharding import Mesh, PartitionSpec as P


SIZES = (4, 2, 8, 2, 2)
AXES = ("y", "l", "z", "h", "c")
SLABS = 8
ROWS = 8
NY = 256
NZ = 128
HALF = ROWS // 2
CY = NY // 2
PAD = 8
CHUNK = 64
FINE = 0.15
COARSE = 0.3
TABLE = (1.0, 0.72, 0.52, 0.37, 0.26, 0.18, 0.13, 0.09)

BLOCKS = 16
YB = CY // BLOCKS
YM = 14
WM = 16
YW = YB + 2 * YM
XH = 14
XW = 12 + 2 * XH
XALL = 48
KEEP = (8, 8, 6, 4, 4, 4, 2)
YCUT = (0, 2, 4, 6, 8, 10, 12)
WIDE = tuple(YW - 2 * cut for cut in YCUT)
STARTS = tuple(sum(KEEP[i] * WIDE[i] for i in range(j)) for j in range(8))
NSEND = STARTS[7]
KW = YB + 2 * WM
OFF = WM - YM

EK, EU, E1, EDGE = 0, 256, 512, 768
EKC, EUC, E1C, CEDGE = 0, 128, 256, 384

F32 = jnp.float32


def up_lane(x):
    return pltpu.roll(x, NZ - 1, axis=x.ndim - 1)


def down_lane(x):
    return pltpu.roll(x, 1, axis=x.ndim - 1)


def lanes(shape):
    return lax.broadcasted_iota(jnp.int32, shape, len(shape) - 1)


def lookup(material):
    result = jnp.zeros(material.shape, F32)
    for number in range(8):
        result = jnp.where(material == number, F32(TABLE[number]), result)
    return result


def z_faces(k, weight):
    lane = lanes(k.shape)
    upper = jnp.where(lane == NZ - 1, 0.0, up_lane(k))
    lower = jnp.where(lane == 0, 0.0, down_lane(k))
    above = weight * (k + upper)
    below = weight * (k + lower)
    return jnp.where(lane == NZ - 1, 0.0, above), above + below


def coefficients(kp, r, a, n, wx, wy, wz, below, above):
    k = kp[r, PAD + a : PAD + a + n]
    cyp = wy * (k + kp[r, PAD + a + 1 : PAD + a + n + 1])
    cym = wy * (k + kp[r, PAD + a - 1 : PAD + a + n - 1])
    cz, zsum = z_faces(k, wz)
    diag = 1.0 - (cyp + cym + zsum)
    cx = None
    if below:
        diag = diag - wx * (k + kp[r - 1, PAD + a : PAD + a + n])
    if above:
        cx = wx * (k + kp[r + 1, PAD + a : PAD + a + n])
        diag = diag - cx
    return cx, cyp, cym, cz, diag


def combine(u, r, a, n, cx_below, cx_above, cyp, cym, cz, diag):
    here = u[r, PAD + a : PAD + a + n]
    new = diag * here
    new = new + cyp * u[r, PAD + a + 1 : PAD + a + n + 1]
    new = new + cym * u[r, PAD + a - 1 : PAD + a + n - 1]
    new = new + cz * up_lane(here) + down_lane(cz * here)
    if cx_below is not None:
        new = new + cx_below * u[r - 1, PAD + a : PAD + a + n]
    if cx_above is not None:
        new = new + cx_above * u[r + 1, PAD + a : PAD + a + n]
    return new


def base(u, r, a, n, cx, cyp, cym, cz, diag, below, above):
    s = slice(a, a + n)
    return combine(
        u, r, a, n, cx[r - 1, s] if below else None, cx[r, s] if above else None, cyp[r, s], cym[r, s], cz[r, s], diag[r, s]
    )


def edge_sweep(kp, u, side, rows, a, n, wx, wy, wz):
    r = 0 if side == 0 else rows - 1
    cx, cyp, cym, cz, diag = coefficients(kp, r, a, n, wx, wy, wz, side == 1, side == 0)
    below = wx * (kp[r, PAD + a : PAD + a + n] + kp[r - 1, PAD + a : PAD + a + n]) if side == 1 else None
    return combine(u, r, a, n, below, cx, cyp, cym, cz, diag)


def each_row(count, visit):
    visit(0, False, True)

    def body(r, carry):
        visit(r, True, True)
        return carry

    lax.fori_loop(1, count - 1, body, 0)
    visit(count - 1, True, False)


def pieces(width):
    return [(a, CHUNK) for a in range(0, width, CHUNK)]


def clear_margin(ref, width):
    rows = ref.shape[0]
    ref[:, 0:PAD] = jnp.zeros((rows, PAD, NZ), F32)
    ref[:, PAD + width : PAD + width + PAD] = jnp.zeros((rows, PAD, NZ), F32)


def halve(ref, x, margin):
    total = None
    for p in range(2):
        for q in range(2):
            part = ref[2 * x + p, pl.ds(margin + q, CY, 2), :]
            total = part if total is None else total + part
    return 0.25 * total


FINE_W = (0.5 * FINE, 0.5 * FINE, 0.5 * FINE)
COARSE_W = (0.125 * COARSE, 0.125 * COARSE, 0.5 * COARSE)


def place(name):
    return lax.axis_index(name)


def block_of(h):
    return (place("y") * 2 + place("l")) * 2 + h


def lives():
    index = (place("z") * 2 + place("h")) * 2 + place("c")
    return jnp.where(index > 0, F32(1), F32(0)), jnp.where(index < 31, F32(1), F32(0))


EDGES = (0, 7, 1, 6)
ALL_ROWS = tuple(range(ROWS))


def start_rows(rows, u_in, mat, up, numbers, u_sem, m_sem):
    for r in rows:
        pltpu.make_async_copy(mat.at[r], numbers.at[r], m_sem.at[r]).start()
        pltpu.make_async_copy(u_in.at[0, r], up.at[r, pl.ds(PAD, NY)], u_sem.at[r]).start()


def take_rows(rows, u_in, mat, kp, up, numbers, u_sem, m_sem):
    clear_margin(kp, NY)
    clear_margin(up, NY)
    for r in rows:
        pltpu.make_async_copy(mat.at[r], numbers.at[r], m_sem.at[r]).wait()
        for a, n in pieces(NY):
            kp[r, PAD + a : PAD + a + n] = lookup(numbers[r, a : a + n])
    for r in rows:
        pltpu.make_async_copy(u_in.at[0, r], up.at[r, pl.ds(PAD, NY)], u_sem.at[r]).wait()


def first_kernel(u_in, mat, src, sc, so, kp, up, edge, numbers, ends, u_sem, m_sem, s_sem):
    start_rows(EDGES, u_in, mat, up, numbers, u_sem, m_sem)
    for side, r in ((0, 0), (1, ROWS - 1)):
        pltpu.make_async_copy(src.at[r], ends.at[side], s_sem.at[side]).start()
    take_rows(EDGES, u_in, mat, kp, up, numbers, u_sem, m_sem)
    for side, r in ((0, 0), (1, ROWS - 1)):
        pltpu.make_async_copy(src.at[r], ends.at[side], s_sem.at[side]).wait()
        for a, n in pieces(NY):
            edge[side, EK + a : EK + a + n] = kp[r, PAD + a : PAD + a + n]
            edge[side, EU + a : EU + a + n] = up[r, PAD + a : PAD + a + n]
            edge[side, E1 + a : E1 + a + n] = edge_sweep(kp, up, side, ROWS, a, n, *FINE_W) + FINE * ends[side, a : a + n]
    c = place("c")
    sc[...] = edge[1 - c]
    so[...] = edge[c]


def coef_kernel(
    u_in, mat, src_in, _, cx, cyp, cym, cz, dg, ccx, ccyp, ccym, ccz, cdg, b1, b2, cb1, ucp, csc, cso, strip, strip_h, up, src,
    kw, kcp, edge, kp, numbers, u_sem, m_sem, s_sem,
):
    start_rows(ALL_ROWS, u_in, mat, up, numbers, u_sem, m_sem)
    for r in range(ROWS):
        pltpu.make_async_copy(src_in.at[r], src.at[r], s_sem.at[r]).start()
    take_rows(ALL_ROWS, u_in, mat, kp, up, numbers, u_sem, m_sem)
    for r in range(ROWS):
        pltpu.make_async_copy(src_in.at[r], src.at[r], s_sem.at[r]).wait()
    clear_margin(kcp, CY)
    clear_margin(ucp, CY)
    for x in range(HALF):
        kcp[x, PAD : PAD + CY] = halve(kp, x, PAD)
        ucp[x, PAD : PAD + CY] = halve(up, x, PAD)
    clear_margin(b1, NY)
    clear_margin(b2, NY)
    clear_margin(cb1, CY)
    kw[:, 0:WM] = jnp.zeros((HALF, WM, NZ), F32)
    kw[:, WM + CY : WM + CY + WM] = jnp.zeros((HALF, WM, NZ), F32)
    kw[:, WM : WM + CY] = kcp[:, PAD : PAD + CY]
    h = place("h")
    strip[...] = kw[:, pl.ds(pl.multiple_of(block_of(h) * YB, 8), KW)]
    strip_h[...] = kw[:, pl.ds(pl.multiple_of(block_of(1 - h) * YB, 8), KW)]

    def make(k, u, n_all, weights, outs, target, source):
        fx, fyp, fym, fz, fd = outs

        def visit(r, below, above):
            for a, n in pieces(n_all):
                s = slice(a, a + n)
                wx = weights[0]
                above_c, yp, ym, zc, dd = coefficients(k, r, a, n, *weights, below, above)
                fyp[r, s], fym[r, s], fz[r, s], fd[r, s] = yp, ym, zc, dd
                if above:
                    fx[r, s] = above_c
                under = wx * (k[r, PAD + a : PAD + a + n] + k[r - 1, PAD + a : PAD + a + n]) if below else None
                new = combine(u, r, a, n, under, above_c, yp, ym, zc, dd)
                if source is not None:
                    new = new + FINE * source[r, s]
                target[r, PAD + a : PAD + a + n] = new

        each_row(u.shape[0], visit)

    make(kp, up, NY, FINE_W, (cx, cyp, cym, cz, dg), b1, src)
    inner_rows(b2, b1, (cx, cyp, cym, cz, dg), src)
    make(kcp, ucp, CY, COARSE_W, (ccx, ccyp, ccym, ccz, cdg), cb1, None)
    c = place("c")
    for side, x in ((0, 0), (1, HALF - 1)):
        edge[side, EKC : EKC + CY] = kcp[x, PAD : PAD + CY]
        edge[side, EUC : EUC + CY] = ucp[x, PAD : PAD + CY]
        edge[side, E1C : E1C + CY] = cb1[x, PAD : PAD + CY]
    csc[...] = edge[1 - c]
    cso[...] = edge[c]


def inner_rows(dst, src_ref, coefs, source):
    def body(r, carry):
        for a, n in pieces(NY):
            dst[r, PAD + a : PAD + a + n] = base(src_ref, r, a, n, *coefs, True, True) + FINE * source[r, a : a + n]
        return carry

    lax.fori_loop(2, ROWS - 2, body, 0)


def outer_rows(dst, src_ref, store, face, coefs, source):
    for r in (1, ROWS - 2, 0, ROWS - 1):
        below, above = r > 0, r < ROWS - 1
        for a, n in pieces(NY):
            new = base(src_ref, r, a, n, *coefs, below, above) + FINE * source[r, a : a + n]
            here = src_ref[r, PAD + a : PAD + a + n]
            if not below:
                new = new + face(0, a, n) * (store[0, a : a + n] - here)
            if not above:
                new = new + face(1, a, n) * (store[1, a : a + n] - here)
            dst[r, PAD + a : PAD + a + n] = new


def fix_rows(target, old, halo, face, rows, width):
    for side, r in ((0, 0), (1, rows - 1)):
        for a, n in pieces(width):
            s = slice(PAD + a, PAD + a + n)
            target[r, s] = target[r, s] + face(side, a, n) * (halo(side, a, n) - old[r, s])


def halo_after(store, old, halo, later, face, live, rows, width):
    for side, r in ((0, 0), (1, rows - 1)):
        for a, n in pieces(width):
            flux = face(side, a, n) * (old[r, PAD + a : PAD + a + n] - halo(side, a, n))
            store[side, a : a + n] = live[side] * (later(side, a, n) + flux)


def full_sweep(dst, src_ref, store, face, rows, width, coefs, source):
    def visit(r, below, above):
        for a, n in pieces(width):
            new = base(src_ref, r, a, n, *coefs, below, above)
            if source is not None:
                new = new + FINE * source[r, a : a + n]
            here = src_ref[r, PAD + a : PAD + a + n]
            if not below:
                new = new + face(0, a, n) * (store[0, a : a + n] - here)
            if not above:
                new = new + face(1, a, n) * (store[1, a : a + n] - here)
            dst[r, PAD + a : PAD + a + n] = new

    each_row(rows, visit)


def reader(ref, offset=0):
    return lambda side, a, n: ref[side, offset + a : offset + a + n]


def second_kernel(
    src, sc, so, rc, ro, up, b1, b2, cx, cyp, cym, cz, dg, u1, u2, faces, tc, to, own, got, store, edge,
):
    c = place("c")
    live = lives()
    own[1 - c] = sc[...]
    own[c] = so[...]
    got[1 - c] = rc[...]
    got[c] = ro[...]
    for side in range(2):
        got[side] = got[side] * live[side]
        for a, n in pieces(NY):
            faces[side, a : a + n] = (0.5 * FINE) * (own[side, EK + a : EK + a + n] + got[side, EK + a : EK + a + n])
    halo_after(store, up, reader(got, EU), reader(got, E1), reader(faces), live, ROWS, NY)
    fix_rows(u1, up, reader(got, EU), reader(faces), ROWS, NY)
    coefs = (cx, cyp, cym, cz, dg)
    outer_rows(u2, u1, store, reader(faces), coefs, src)
    for side, r in ((0, 0), (1, ROWS - 1)):
        for a, n in pieces(NY):
            edge[side, a : a + n] = u2[r, PAD + a : PAD + a + n]
            edge[side, NY + a : NY + a + n] = base(u2, r, a, n, *coefs, side == 1, side == 0) + FINE * src[r, a : a + n]
    tc[...] = edge[1 - c]
    to[...] = edge[c]


def middle_kernel(
    u2, src, csc, cso, crc, cro, ucp, cb1, cx, cyp, cym, cz, dg, ccx, ccyp, ccym, ccz, cdg, b3, b4, au, own, got, cfaces, cstore, c1,
):
    c = place("c")
    live = lives()
    own[1 - c] = csc[...]
    own[c] = cso[...]
    got[1 - c] = crc[...]
    got[c] = cro[...]
    for side in range(2):
        got[side] = got[side] * live[side]
        for a, n in pieces(CY):
            cfaces[side, a : a + n] = (0.125 * COARSE) * (own[side, EKC + a : EKC + a + n] + got[side, EKC + a : EKC + a + n])
    halo_after(cstore, ucp, reader(got, EUC), reader(got, E1C), reader(cfaces), live, HALF, CY)
    c1[...] = cb1[...]
    fix_rows(c1, ucp, reader(got, EUC), reader(cfaces), HALF, CY)
    clear_margin(b3, NY)
    clear_margin(b4, NY)
    clear_margin(au, CY)

    def visit(r, below, above):
        for a, n in pieces(NY):
            b3[r, PAD + a : PAD + a + n] = base(u2, r, a, n, cx, cyp, cym, cz, dg, below, above) + FINE * src[r, a : a + n]

    each_row(ROWS, visit)
    inner_rows(b4, b3, (cx, cyp, cym, cz, dg), src)
    full_sweep(au, c1, cstore, reader(cfaces), HALF, CY, (ccx, ccyp, ccym, ccz, cdg), None)


def third_kernel(
    u2, src, faces, rc, ro, b3, b4, au, cx, cyp, cym, cz, dg, u3, f, h_out, strips, got, store, wp,
):
    c = place("c")
    live = lives()
    got[1 - c] = rc[...]
    got[c] = ro[...]
    for side in range(2):
        got[side] = got[side] * live[side]
    halo_after(store, u2, reader(got), reader(got, NY), reader(faces), live, ROWS, NY)
    fix_rows(u3, u2, reader(got), reader(faces), ROWS, NY)
    outer_rows(f, u3, store, reader(faces), (cx, cyp, cym, cz, dg), src)
    keep = jnp.where(place("y") + place("l") > 0, F32(1), F32(0))
    wp[:, 0:WM] = jnp.zeros((HALF, WM, NZ), F32)
    wp[:, WM + CY : WM + CY + WM] = jnp.zeros((HALF, WM, NZ), F32)
    for x in range(HALF):
        coarse = keep * au[x, PAD : PAD + CY]
        total = None
        for p in range(2):
            for q in range(2):
                part = f[2 * x + p, pl.ds(PAD + q, CY, 2), :] - coarse
                h_out[2 * x + p, pl.ds(q, CY, 2), :] = part
                total = part if total is None else total + part
        wp[x, WM : WM + CY] = 0.25 * total
    for b in range(BLOCKS):
        for x in range(HALF):
            strips[b, x * YW : (x + 1) * YW] = wp[x, b * YB + WM - YM : b * YB + WM - YM + YW]


def merge_kernel(strip, strip_h, kown):
    h = place("h")
    kown[pl.ds(4 * h, HALF)] = strip[...]
    kown[pl.ds(4 * (1 - h), HALF)] = strip_h[...]


def pack_kernel(own, kown, keven, kodd, even, odd, kall):
    kall[0:8] = kown[...]
    kall[8:16] = keven[...]
    kall[16:24] = kodd[...]
    up = 1 - lax.rem(place("z"), 2)
    for j in range(7):
        n, cut, wide = KEEP[j], YCUT[j], WIDE[j]
        for t in range(n):
            at = STARTS[j] + t * wide
            high = own[j, (8 - n + t) * YW + cut : (8 - n + t) * YW + cut + wide]
            low = own[j, t * YW + cut : t * YW + cut + wide]
            even[at : at + wide] = jnp.where(up == 1, high, low)
            odd[at : at + wide] = jnp.where(up == 1, low, high)


def position(i):
    return 8 * (i // 4) + i % 4


def patch_kernel(kall, pkall, cxp, cyp, cym, cz, dg, kp):
    c = place("c")
    z = place("z")
    is_up = 1 - lax.rem(z, 2)
    low = jnp.where(z > 0, F32(1), F32(0))
    high = jnp.where(z < 7, F32(1), F32(0))
    first = 4 * c + 16 - XH
    kp[:, 0:PAD] = jnp.zeros((XALL, PAD, NZ), F32)
    kp[:, PAD + KW : PAD + KW + PAD] = jnp.zeros((XALL, PAD, NZ), F32)
    for core, k_ref in ((c, kall), (1 - c, pkall)):
        shift = 16 + 4 * core
        for i in range(8):
            kp[shift + position(i), PAD : PAD + KW] = k_ref[i]

            kp[shift + position(i) - 16, PAD : PAD + KW] = k_ref[8 * (1 + is_up) + i] * low
            kp[shift + position(i) + 16, PAD : PAD + KW] = k_ref[8 * (2 - is_up) + i] * high

    ycell = block_of(place("h")) * YB - WM + lax.broadcasted_iota(jnp.int32, (KW, NZ), 0)
    ymask = jnp.where((ycell >= 0) & (ycell < CY), F32(1), F32(0))
    wx, _, wz = COARSE_W

    def coef(g, carry):
        for t in range(4):
            r = 4 * g + t
            q = first + r
            k = kp[q, PAD : PAD + KW]
            a = wx * (k + kp[q, PAD + 1 : PAD + KW + 1])
            b = wx * (k + kp[q, PAD - 1 : PAD + KW - 1])
            zc, zsum = z_faces(k, wz)
            above = wx * (k + kp[q + 1, PAD : PAD + KW])
            below = wx * (k + kp[q - 1, PAD : PAD + KW])
            row = 16 * z + 4 * c - XH + r
            m = ymask * jnp.where((row >= 0) & (row < CY), F32(1), F32(0))
            m_above = ymask * jnp.where((row >= 0) & (row < CY - 1), F32(1), F32(0))
            cyp[r] = a * m
            cym[r] = b * m
            cz[r] = zc * m
            cxp[r] = above * m_above
            dg[r] = (1.0 - (a + b + zsum + above + below)) * m
        return carry

    lax.fori_loop(0, XW // 4, coef, 0)


def chain_kernel(own, part, even, odd, peven, podd, cxp, cyp, cym, cz, dg, out, w, ea, eb):
    c = place("c")
    z = place("z")
    is_up = lax.rem(z, 2) == 0
    low = jnp.where(z > 0, F32(1), F32(0))
    high = jnp.where(z < 7, F32(1), F32(0))
    first = 4 * c + 16 - XH

    for core, mine, e_ref, o_ref in ((c, own, even, odd), (1 - c, part, peven, podd)):
        shift = 16 + 4 * core
        for j in range(7):
            for i in range(8):
                w[j, shift + position(i), OFF : OFF + YW] = mine[j, i * YW : (i + 1) * YW]

        def fill(from_below, from_above):
            for j in range(7):
                n, cut, wide = KEEP[j], YCUT[j], WIDE[j]
                for t in range(n):
                    at = STARTS[j] + t * wide
                    w[j, shift + position(8 - n + t) - 16, OFF + cut : OFF + cut + wide] = from_below[at : at + wide] * low
                    w[j, shift + position(t) + 16, OFF + cut : OFF + cut + wide] = from_above[at : at + wide] * high

        @pl.when(is_up)
        def _():
            fill(o_ref, e_ref)

        @pl.when(jnp.logical_not(is_up))
        def _():
            fill(e_ref, o_ref)

    for r in range(XW):
        ea[r, PAD : PAD + KW] = w[0, first + r]

    def each(lo, hi, visit):
        for r in range(lo, hi):
            visit(r)

    def sweep(src, dst, number):
        cut = 0 if number <= 5 else 8
        s = slice(cut, KW - cut)
        n = KW - 2 * cut

        def visit(r):
            here = src[r, PAD + cut : PAD + cut + n]
            zc = cz[r, s]
            new = dg[r, s] * here + cyp[r, s] * src[r, PAD + cut + 1 : PAD + cut + n + 1]
            new = new + cym[r, s] * src[r, PAD + cut - 1 : PAD + cut + n - 1]
            new = new + (cxp[r - 1, s] * src[r - 1, PAD + cut : PAD + cut + n] + cxp[r, s] * src[r + 1, PAD + cut : PAD + cut + n])
            dst[r, PAD + cut : PAD + cut + n] = new + (zc * up_lane(here) + down_lane(zc * here))

        each(number, XW - number, visit)

    out[2:4] = jnp.zeros((2, HALF, YB, NZ), F32)
    for k in range(1, 8):
        sweep(ea, eb, 2 * k - 1)
        sweep(eb, ea, 2 * k)
        m = (k + 1) % SLABS
        for side in range(2):
            for i in range(HALF):
                out[2 * m + side, i] = ea[XH + 8 * side + i, PAD + WM : PAD + WM + YB]
        if k < 7:
            cut = 8 if k >= 3 else 0
            s = slice(PAD + cut, PAD + KW - cut)

            def add(r):
                ea[r, s] = ea[r, s] + w[k, first + r, cut : KW - cut]

            each(2 * k, XW - 2 * k, add)


def last_kernel(h_in, y_in, out):
    for x in range(HALF):
        fix = y_in[:, x].reshape(CY, NZ)
        for p in range(2):
            for q in range(2):
                out[0, 2 * x + p, pl.ds(q, CY, 2), :] = h_in[2 * x + p, pl.ds(q, CY, 2), :] + fix


def call(kernel, outs, scratch, *operands, limit=6, specs=None, alias=()):
    vmem = pl.BlockSpec(memory_space=pltpu.VMEM)
    return pl.pallas_call(
        kernel,
        out_shape=[jax.ShapeDtypeStruct(s, F32) for s in outs],
        in_specs=specs or [vmem] * len(operands),
        out_specs=[vmem] * len(outs),
        scratch_shapes=[s if callable(getattr(s, "get_ref_aval", None)) else pltpu.VMEM(s, F32) for s in scratch],
        input_output_aliases=dict(alias),
        compiler_params=pltpu.CompilerParams(vmem_limit_bytes=limit * 1024 * 1024),
    )(*operands)


def pairs(n, odd):
    found = []
    for i in range(odd, n - 1, 2):
        found += [(i, i + 1), (i + 1, i)]
    if odd:
        found += [(0, n - 1), (n - 1, 0)]
    return found


SPACE = ("z", "h", "c")
PLANE = ("y", "l", "h")


def steps(starts, material, source):
    fine = (ROWS, NY, NZ)
    crs = (HALF, CY, NZ)
    padded = (ROWS, NY + 2 * PAD, NZ)
    cpad = (HALF, CY + 2 * PAD, NZ)
    strip_shape = (HALF, KW, NZ)

    def swap_c(x):
        return lax.ppermute(x, "c", pairs(2, 0))

    def swap_o(x):
        return lax.ppermute(x, SPACE, pairs(32, 1))

    dma = pltpu.SemaphoreType.DMA
    in_hbm = [pl.BlockSpec(memory_space=pltpu.HBM)] * 3
    inputs = [pltpu.with_memory_space_constraint(x, pltpu.HBM) for x in (starts, material, source)]
    numbers = pltpu.VMEM(fine, jnp.int32)
    sc, so = call(
        first_kernel, ((EDGE, NZ), (EDGE, NZ)),
        (padded, padded, (2, EDGE, NZ), numbers, (2, NY, NZ), dma((ROWS,)), dma((ROWS,)), dma((2,))),
        *inputs, specs=in_hbm,
    )
    ro = swap_o(so)
    rc = swap_c(sc)
    edges = (CEDGE, NZ)
    *coefs, b1, b2, cb1, ucp, csc, cso, strip, strip_h, up, source = call(
        coef_kernel,
        (fine,) * 5 + (crs,) * 5 + (padded, padded, cpad, cpad, edges, edges, strip_shape, strip_shape, padded, fine),
        ((HALF, CY + 2 * WM, NZ), cpad, (2, CEDGE, NZ), padded, numbers, dma((ROWS,)), dma((ROWS,)), dma((ROWS,))),
        *inputs, sc, specs=in_hbm + [pl.BlockSpec(memory_space=pl.ANY)], limit=8,
    )
    crc = swap_c(csc)
    cro = swap_o(cso)
    _, u2, faces, tc, to = call(
        second_kernel,
        (padded, padded, (2, NY, NZ), (2 * NY, NZ), (2 * NY, NZ)),
        ((2, EDGE, NZ), (2, EDGE, NZ), (2, NY, NZ), (2, 2 * NY, NZ)),
        source, sc, so, rc, ro, up, b1, b2, *coefs[:5], alias=((6, 0), (7, 1)),
    )
    ro2 = swap_o(to)
    rc2 = swap_c(tc)
    strip_h = lax.ppermute(strip_h, "h", pairs(2, 0))
    b3, b4, au = call(
        middle_kernel, (padded, padded, cpad), ((2, CEDGE, NZ), (2, CEDGE, NZ), (2, CY, NZ), (2, CY, NZ), cpad),
        u2, source, csc, cso, crc, cro, ucp, cb1, *coefs,
    )
    _, _, moved, strips = call(
        third_kernel,
        (padded, padded, fine, (BLOCKS, HALF * YW, NZ)),
        ((2, 2 * NY, NZ), (2, NY, NZ), (HALF, CY + 2 * WM, NZ)),
        u2, source, faces, rc2, ro2, b3, b4, au, *coefs[:5], alias=((5, 0), (6, 1)),
    )
    own = lax.all_to_all(strips, PLANE, 0, 0, tiled=True)
    strip, _ = lax.optimization_barrier((strip, strips))
    (kown,) = call(merge_kernel, ((8, KW, NZ),), (), strip, strip_h)
    keven = lax.ppermute(kown, "z", pairs(8, 0))
    kodd = lax.ppermute(kown, "z", pairs(8, 1))
    own, moved = lax.optimization_barrier((own, moved))
    own = own.reshape(SLABS, 8 * YW, NZ)
    even, odd, kall = call(pack_kernel, ((NSEND, NZ), (NSEND, NZ), (24, KW, NZ)), (), own, kown, keven, kodd)
    even = lax.ppermute(even, "z", pairs(8, 0))
    odd = lax.ppermute(odd, "z", pairs(8, 1))
    part = swap_c(own)
    pkall = swap_c(kall)
    moved = lax.ppermute(moved, ("y", "l"), [(i, (i + 1) % 8) for i in range(8)])
    peven = swap_c(even)
    podd = swap_c(odd)
    dom = (XW + 1, KW + 2 * PAD, NZ)
    flat = (XW, KW, NZ)
    patch = call(patch_kernel, (flat,) * 5, ((XALL, KW + 2 * PAD, NZ),), kall, pkall)
    (fixes,) = call(
        chain_kernel, ((BLOCKS, HALF, YB, NZ),), ((7, XALL, KW, NZ), dom, dom),
        own, part, even, odd, peven, podd, *patch, limit=12,
    )
    fixes = lax.all_to_all(fixes, PLANE, 0, 0, tiled=True)
    (result,) = call(last_kernel, ((1, ROWS, NY, NZ),), (), moved, fixes)
    return result


def solution(mesh):
    refined = Mesh(mesh.devices.reshape(SIZES), AXES)
    in_specs = (P(("y", "l"), SPACE, None, None), P(SPACE, None, None), P(SPACE, None, None))
    out_specs = P(("y", "l"), SPACE, None, None)
    return jax.shard_map(steps, mesh=refined, in_specs=in_specs, out_specs=out_specs, check_vma=False)
```
